256 devices in a mesh: det: 64 (over x, z, core), head: 4 (over y).
Axes of the slice: x: 4, y: 4, z: 8, core: 2. Of those that a mesh axis runs over, the one named last changes fastest.
Arguments:
- elements: bfloat16 [32768, 1024], P('det'), may hold values from -6 to 6
- element_types: int32 [32768], P('det'), may hold values from 0 to 1, as said below
- handover_counts: int32 [64, 64], replicated, may hold values from 0 to 16, as said below
- block_lists: int32 [256, 16], P('det'), may hold values from 0 to 255, as said below
- w_first: bfloat16 [2, 1024, 2048], P(None, None, 'head'), may hold values from -0.1875 to 0.1875
- w_second: bfloat16 [2, 2048, 1024], P(None, 'head'), may hold values from -0.125 to 0.125
- w_query: bfloat16 [1024, 1024], P(None, 'head'), may hold values from -3 to 3
- key_value_weight: bfloat16 [1024, 2, 256], P(None, None, 'head'), may hold values from -0.1875 to 0.1875
- attention_cotangent: bfloat16 [32768, 1024], P('det', 'head'), may hold values from -6 to 6
Outputs:
- attended: bfloat16 [32768, 1024], P('det', 'head')
- x_grad: bfloat16 [32768, 1024], P('det', 'head')
The draws below stay inside these ranges and needn't reach their ends.
Inputs may be any that keep to these rules, and one draw needn't show every extreme that they name: `element_types`: of the 512 elements of each device of det, exactly 256 are of each type. `handover_counts`: row d, column e counts the elements that device d of det hands to device e; every row and every column sums to 512; some entries equal 16. `block_lists`: key block k is held by device k // 4 of det; the 16 entries of a query block may repeat; the lists of the 4 query blocks of one device together name exactly 1 block, counted with repeats, held by each device of det.
All inputs are finite; a program needn't handle non-finite values.
Results may differ from the reference program's by a relative error of at most 0.024.
The reference program's roundings to bfloat16 on the way count: a program that leaves them out, or rounds other values in their place, can miss the bound.
Values may be sent and summed in bfloat16 or wider, within the bound.
A program may use at most 64 MiB of HBM per device.

```python
import jax
import jax.numpy as jnp
from jax import lax

FEATURE_WIDTH = 1024
FFN = 2048
TYPES = 2
KEY_HEADS = 4
HEAD_SIZE = 64
BLOCK_ROWS = 128
LISTED_COUNT = 16
TOK_DEV = 512
ELEMENT_TOTAL = 32768
GROUP_HEADS = 4
QW = 1024
QB_DEV = 4
BLOCK_TOTAL = 256
N_DET = 64


def shuffle_types(subkey):
    base = jnp.arange(TOK_DEV, dtype=jnp.int32) % TYPES
    return jax.random.permutation(subkey, base)


def draw_element_types(key, part):
    keys_all = jax.random.split(jax.random.fold_in(key, 7), N_DET)
    return jax.vmap(shuffle_types)(keys_all).reshape(ELEMENT_TOTAL).astype(jnp.int32)


def draw_handover_counts(key, part):
    per_peer = TOK_DEV // N_DET
    key_first, key_second, key_third = jax.random.split(key, 3)
    recv_perm = jax.random.permutation(key_first, N_DET)
    send_perm = jax.random.permutation(key_second, N_DET)
    spread = jax.random.randint(key_third, (N_DET // 2,), 0, per_peer)
    spread = spread.at[0].set(per_peer)
    amounts = jnp.stack([per_peer + spread, per_peer - spread], axis=1).reshape(N_DET)
    diagonal_ids = (recv_perm[None, :] - send_perm[:, None]) % N_DET
    return amounts[diagonal_ids].astype(jnp.int32)


def owner_order(subkey):
    return jax.random.permutation(subkey, N_DET)


def draw_block_lists(key, part):
    slot_count = QB_DEV * LISTED_COUNT
    key_first, key_second = jax.random.split(key)
    orders = jax.vmap(owner_order)(jax.random.split(key_first, N_DET))
    owners = jnp.tile(orders, (1, slot_count // N_DET))
    local_ids = jax.random.randint(key_second, (N_DET, slot_count), 0, QB_DEV)
    return (owners * QB_DEV + local_ids).reshape(N_DET * QB_DEV, LISTED_COUNT).astype(jnp.int32)


def draw_w_query(key, part):
    drawn = jax.random.normal(key, (FEATURE_WIDTH, QW), jnp.float32) * FEATURE_WIDTH ** (-0.5)
    return jnp.clip(drawn, -3.0, 3.0).astype(jnp.bfloat16)


def block_levels(rng, dims, cuts, low, largest):
    def one(dim, shards_of):
        heights = jax.random.uniform(jax.random.fold_in(jax.random.fold_in(rng, 6), dim), (shards_of,), jnp.float32, low / len(cuts), largest / len(cuts))
        return jnp.repeat(jnp.exp(heights), dims[dim] // shards_of).reshape((-1,) + (1,) * (len(dims) - dim - 1))

    gain = one(*cuts[0])
    for cut in cuts[1:]:
        gain = gain * one(*cut)
    return gain


def bell_draw(stream_key, dims, width, bound, cuts=(), kind=jnp.bfloat16):
    gain = block_levels(stream_key, dims, cuts, -0.22, 0.18) if cuts else 1.0
    values = jax.random.normal(stream_key, dims, jnp.float32) * width * gain
    return jnp.minimum(jnp.maximum(values, -bound), bound).astype(kind)


def setup_inputs(seed: int = 0) -> dict:
    arg_keys = jax.random.split(jax.random.key(seed), 10)
    return {
        "elements": bell_draw(arg_keys[0], (ELEMENT_TOTAL, FEATURE_WIDTH), 1.0, 6.0, ((0, 64),)),
        "element_types": draw_element_types(jax.random.fold_in(arg_keys[9], 71), 0),
        "handover_counts": draw_handover_counts(jax.random.fold_in(arg_keys[9], 71), 0),
        "block_lists": draw_block_lists(jax.random.fold_in(arg_keys[9], 71), 0),
        "w_first": bell_draw(arg_keys[4], (TYPES, FEATURE_WIDTH, FFN), FEATURE_WIDTH ** -0.5, 0.1875, ((2, 4),)),
        "w_second": bell_draw(arg_keys[5], (TYPES, FFN, FEATURE_WIDTH), FFN ** -0.5, 0.125, ((1, 4),)),
        "w_query": draw_w_query(jax.random.fold_in(arg_keys[9], 71), 0),
        "key_value_weight": bell_draw(arg_keys[7], (FEATURE_WIDTH, 2, KEY_HEADS * HEAD_SIZE), FEATURE_WIDTH ** -0.5, 0.1875, ((2, 4),)),
        "attention_cotangent": bell_draw(arg_keys[8], (ELEMENT_TOTAL, QW), 1.0, 6.0, ((0, 64), (1, 4))),
    }


def to_half(value):
    return lax.optimization_barrier(value.astype(jnp.bfloat16))

def handover_positions(handover_counts):
    starts = jnp.cumsum(handover_counts, axis=1, dtype=jnp.int32) - handover_counts
    offsets = jnp.cumsum(handover_counts, axis=0, dtype=jnp.int32) - handover_counts
    end_rows = starts + handover_counts
    element_ids = jnp.arange(ELEMENT_TOTAL, dtype=jnp.int32)
    source = element_ids // TOK_DEV
    within = element_ids % TOK_DEV
    target = lax.optimization_barrier(jnp.sum((end_rows[source] <= within[:, None]).astype(jnp.int32), axis=1, dtype=jnp.int32))
    return target * TOK_DEV + offsets[source, target] + within - starts[source, target]

def attend(query_block_one, cotangent_block, key_block_rows, value_block_rows):
    score_scaling = HEAD_SIZE ** (-0.5)
    query_expanded = query_block_one.astype(jnp.float32)
    cotangent_wide = cotangent_block.astype(jnp.float32)
    key_expanded = key_block_rows.astype(jnp.float32)
    value_expanded = value_block_rows.astype(jnp.float32)
    score_matrix = jnp.einsum('oenl,iel->enoi', query_expanded, key_expanded) * score_scaling
    row_max = lax.optimization_barrier(jnp.max(score_matrix, axis=-1, keepdims=True))
    exp_scores = jnp.exp(score_matrix - row_max)
    probability = exp_scores / lax.optimization_barrier(jnp.sum(exp_scores, axis=-1, keepdims=True))
    probability_bfloat = to_half(probability)
    attended = jnp.einsum('vnys,svx->yvnx', probability_bfloat.astype(jnp.float32), value_expanded).astype(jnp.bfloat16)
    probability_gradient = jnp.einsum('oenl,iel->enoi', cotangent_wide, value_expanded)
    row_delta = lax.optimization_barrier(jnp.sum(probability * probability_gradient, axis=-1, keepdims=True))
    score_gradient = to_half(probability * (probability_gradient - row_delta)).astype(jnp.float32)
    query_gradient = (jnp.einsum('vnys,svx->yvnx', score_gradient, key_expanded) * score_scaling).astype(jnp.bfloat16)
    key_gradient = jnp.einsum('njtw,tnjs->wns', score_gradient, query_expanded) * score_scaling
    value_gradient = jnp.einsum('njtw,tnjs->wns', probability_bfloat.astype(jnp.float32), cotangent_wide)
    return (attended, query_gradient, key_gradient, value_gradient)

def reference(elements, element_types, handover_counts, block_lists, w_first, w_second, w_query, key_value_weight, attention_cotangent):
    onehot = (element_types[:, None] == jnp.arange(TYPES, dtype=jnp.int32)[None, :]).astype(jnp.float32)
    preact = jnp.einsum('rd,tdh->rth', elements.astype(jnp.float32), w_first.astype(jnp.float32))
    hidden = to_half(jax.nn.gelu(preact) * onehot[:, :, None])
    mlp_sum = jnp.einsum('rth,thd->rd', hidden.astype(jnp.float32), w_second.astype(jnp.float32))
    mixed = (elements.astype(jnp.float32) + mlp_sum).astype(jnp.bfloat16)
    position = handover_positions(handover_counts)
    moved = jnp.zeros_like(mixed).at[position].set(mixed)
    query_rows_all = jnp.dot(moved, w_query, preferred_element_type=jnp.float32).astype(jnp.bfloat16)
    key_value_flat = key_value_weight.reshape(FEATURE_WIDTH, 2 * KEY_HEADS * HEAD_SIZE)
    key_value_pairs = jnp.dot(moved, key_value_flat, preferred_element_type=jnp.float32).astype(jnp.bfloat16)
    key_value_blocks = key_value_pairs.reshape(BLOCK_TOTAL, BLOCK_ROWS, 2, KEY_HEADS, HEAD_SIZE)
    query_block_list = query_rows_all.reshape(BLOCK_TOTAL, BLOCK_ROWS, KEY_HEADS, GROUP_HEADS, HEAD_SIZE)
    cotangent_blocks = attention_cotangent.reshape(BLOCK_TOTAL, BLOCK_ROWS, KEY_HEADS, GROUP_HEADS, HEAD_SIZE)

    def block_step(running, inputs):
        query_block_one, cotangent_block, listed_block_index = inputs
        key_value_rows = key_value_blocks[listed_block_index].reshape(LISTED_COUNT * BLOCK_ROWS, 2, KEY_HEADS, HEAD_SIZE)
        attended, query_gradient, key_gradient, value_gradient = attend(query_block_one, cotangent_block, key_value_rows[:, 0], key_value_rows[:, 1])
        slot_gradients = jnp.stack([key_gradient, value_gradient], axis=1).reshape(LISTED_COUNT, BLOCK_ROWS, 2 * KEY_HEADS * HEAD_SIZE)
        slot_gradients = to_half(slot_gradients).astype(jnp.float32)
        running = running.at[listed_block_index].add(slot_gradients)
        return (running, (attended, query_gradient))
    empty_gradients = jnp.zeros((BLOCK_TOTAL, BLOCK_ROWS, 2 * KEY_HEADS * HEAD_SIZE), jnp.float32)
    key_gradient_total, (attended, query_gradient) = lax.scan(block_step, empty_gradients, (query_block_list, cotangent_blocks, block_lists))
    key_bfloat = key_gradient_total.reshape(ELEMENT_TOTAL, 2 * KEY_HEADS * HEAD_SIZE).astype(jnp.bfloat16)
    upstream_att = jnp.dot(query_gradient.reshape(ELEMENT_TOTAL, QW), w_query.T, preferred_element_type=jnp.float32)
    upstream_att = upstream_att + jnp.dot(key_bfloat, key_value_flat.T, preferred_element_type=jnp.float32)
    upstream = upstream_att.astype(jnp.bfloat16)[position]
    hidden_grad = jnp.einsum('rd,thd->rth', upstream.astype(jnp.float32), w_second.astype(jnp.float32)) * onehot[:, :, None]
    preact_grad = to_half(jax.vjp(jax.nn.gelu, preact)[1](hidden_grad)[0])
    input_sum = jnp.einsum('rth,tdh->rd', preact_grad.astype(jnp.float32), w_first.astype(jnp.float32))
    x_grad = (upstream.astype(jnp.float32) + input_sum).astype(jnp.bfloat16)
    return (attended.reshape(ELEMENT_TOTAL, QW), x_grad)
```

```python
import functools

import jax
import jax.numpy as jnp
from jax import lax
from jax.experimental import pallas as pl
from jax.experimental.pallas import tpu as pltpu
from jax.sharding import PartitionSpec as P

HEAD_SIZE = 64
BLOCK_ROWS = 128
LISTED_COUNT = 16
GROUP_HEADS = 4
SCALE = HEAD_SIZE ** (-0.5)

F32 = jnp.float32
BF16 = jnp.bfloat16


def dot_nn(a, b):
    return lax.dot_general(a, b, (((1,), (0,)), ((), ())), preferred_element_type=F32)


def dot_nt(a, b):
    return lax.dot_general(a, b, (((1,), (1,)), ((), ())), preferred_element_type=F32)


def dot_tn(a, b):
    return lax.dot_general(a, b, (((0,), (0,)), ((), ())), preferred_element_type=F32)


def attention_kernel(
    list_ref, owner_ref, q_ref, do_ref, kv_hbm, att_ref, dq_ref, grad_ref, kv_buf, score, sems
):
    blocks = q_ref.shape[0] // BLOCK_ROWS
    rows = GROUP_HEADS * BLOCK_ROWS
    pair = 2
    steps = LISTED_COUNT // pair
    keys = pair * BLOCK_ROWS

    for b in range(blocks):

        def start(s, carry, b=b):
            slot = b * LISTED_COUNT + s
            pltpu.make_async_copy(kv_hbm.at[list_ref[slot]], kv_buf.at[slot], sems.at[b]).start()
            return carry

        lax.fori_loop(0, LISTED_COUNT, start, 0)

    def stack(ref, b):
        base = pl.multiple_of(b * BLOCK_ROWS, BLOCK_ROWS)
        tile = ref[pl.ds(base, BLOCK_ROWS), :]
        return jnp.concatenate(
            [tile[:, g * HEAD_SIZE : (g + 1) * HEAD_SIZE] for g in range(GROUP_HEADS)], axis=0
        )

    def unstack(value_t):
        parts = [
            value_t[:, g * BLOCK_ROWS : (g + 1) * BLOCK_ROWS].T for g in range(GROUP_HEADS)
        ]
        return jnp.concatenate(parts, axis=1)

    def one_block(b, carry):
        first = b * LISTED_COUNT
        pltpu.make_async_copy(
            kv_buf.at[pl.ds(first, LISTED_COUNT)], kv_buf.at[pl.ds(first, LISTED_COUNT)], sems.at[b]
        ).wait()
        q = stack(q_ref, b) * jnp.asarray(SCALE, BF16)
        do = stack(do_ref, b)
        none = jnp.zeros_like(q)
        q_pad = jnp.concatenate([q, none], axis=1)
        do_pad = jnp.concatenate([none, do], axis=1)

        def kv_at(i):
            return kv_buf[pl.ds(first + i * pair, pair)].reshape(keys, 2 * HEAD_SIZE)

        def at(i):
            return pl.ds(pl.multiple_of(i * keys, keys), keys)

        def pass_a(i, top):
            s = dot_nt(kv_at(i), q_pad)
            score[at(i), :] = s
            return jnp.maximum(top, jnp.max(s.reshape(keys // 8, 8, rows), axis=0))

        top = lax.fori_loop(0, steps, pass_a, jnp.full((8, rows), -jnp.inf, F32), unroll=2)
        top = jnp.max(top, axis=0, keepdims=True)

        def pass_b(i, carry):
            total, acc = carry
            p = jnp.exp(score[at(i), :] - top)
            score[at(i), :] = p
            total = total + jnp.sum(p.reshape(keys // 8, 8, rows), axis=0)
            acc = acc + dot_tn(kv_at(i), p.astype(BF16))
            return total, acc

        total, acc = lax.fori_loop(
            0,
            steps,
            pass_b,
            (jnp.zeros((8, rows), F32), jnp.zeros((2 * HEAD_SIZE, rows), F32)),
            unroll=2,
        )
        inverse = 1.0 / jnp.sum(total, axis=0, keepdims=True)
        out_t = acc[HEAD_SIZE:, :] * inverse
        base = pl.multiple_of(b * BLOCK_ROWS, BLOCK_ROWS)
        att_ref[pl.ds(base, BLOCK_ROWS), :] = unstack(out_t).astype(att_ref.dtype)
        delta = jnp.sum(out_t * do.astype(F32).T, axis=0, keepdims=True)
        both = jnp.concatenate([q_pad, do_pad], axis=0)

        def pass_c(i, acc):
            prob = score[at(i), :] * inverse
            kv = kv_at(i)
            dp = dot_nt(kv, do_pad)
            ds = (prob * (dp - delta)).astype(BF16)
            acc = acc + dot_tn(kv, ds)
            grads = dot_nn(jnp.concatenate([ds, prob.astype(BF16)], axis=1), both)
            grads = grads.astype(BF16)
            for k in range(pair):
                grad_ref[owner_ref[first + i * pair + k]] = grads[
                    k * BLOCK_ROWS : (k + 1) * BLOCK_ROWS
                ]
            return acc

        acc = lax.fori_loop(0, steps, pass_c, jnp.zeros((2 * HEAD_SIZE, rows), F32), unroll=2)
        dq_t = acc[:HEAD_SIZE, :] * SCALE
        dq_ref[pl.ds(base, BLOCK_ROWS), :] = unstack(dq_t).astype(dq_ref.dtype)
        return carry

    lax.fori_loop(0, blocks, one_block, 0)


def attention(lists, owners, q, do, kv):
    slots = lists.shape[0]
    vm = pl.BlockSpec(memory_space=pltpu.VMEM)
    sm = pl.BlockSpec(memory_space=pltpu.SMEM)
    return pl.pallas_call(
        attention_kernel,
        out_shape=(
            jax.ShapeDtypeStruct(q.shape, BF16),
            jax.ShapeDtypeStruct(q.shape, BF16),
            jax.ShapeDtypeStruct((slots, BLOCK_ROWS, 2 * HEAD_SIZE), BF16),
        ),
        in_specs=[sm, sm, vm, vm, pl.BlockSpec(memory_space=pl.ANY)],
        out_specs=(vm, vm, vm),
        scratch_shapes=[
            pltpu.VMEM((slots, BLOCK_ROWS, 2 * HEAD_SIZE), BF16),
            pltpu.VMEM((LISTED_COUNT * BLOCK_ROWS, GROUP_HEADS * BLOCK_ROWS), F32),
            pltpu.SemaphoreType.DMA((slots // LISTED_COUNT,)),
        ],
        compiler_params=pltpu.CompilerParams(vmem_limit_bytes=40 << 20),
        name="attention",
    )(lists, owners, q, do, kv)


def before(counts):
    ids = jnp.arange(counts.shape[0], dtype=jnp.int32)
    earlier = ids[None, :] < ids[:, None]
    return jnp.sum(jnp.where(earlier, counts[None, :], 0), axis=1, dtype=jnp.int32)


def slot_rows(counts, capacity):
    within = jnp.arange(capacity, dtype=jnp.int32)[None, :]
    rows = jnp.where(within < counts[:, None], before(counts)[:, None] + within, -1)
    return rows.reshape(-1)


def select(slot_row, row_count):
    ids = jnp.arange(row_count, dtype=jnp.int32)
    return (slot_row[:, None] == ids[None, :]).astype(BF16)


def shards(
    elements,
    element_types,
    handover_counts,
    block_lists,
    w_first,
    w_second,
    w_query,
    key_value_weight,
    attention_cotangent,
):
    peers = lax.axis_size("det")
    me = lax.axis_index("det")
    row_count, width = elements.shape
    types = w_first.shape[0]
    share = width // lax.axis_size("head")
    capacity = 2 * row_count // peers
    my_columns = lax.axis_index("head") * share

    send_rows = slot_rows(
        lax.dynamic_index_in_dim(handover_counts, me, 0, keepdims=False), capacity
    )
    recv_rows = slot_rows(
        lax.dynamic_index_in_dim(handover_counts, me, 1, keepdims=False), capacity
    )
    send_pick = select(send_rows, row_count)
    recv_pick = select(recv_rows, row_count)

    blocks = row_count // BLOCK_ROWS
    slots = blocks * LISTED_COUNT
    flat_list = block_lists.reshape(slots)
    owners = flat_list // blocks
    all_lists = lax.all_gather(flat_list, "det", axis=0, tiled=False)
    held = all_lists // blocks == me
    wanted = jnp.sum(jnp.where(held, all_lists % blocks, 0), axis=1, dtype=jnp.int32)

    mask = (element_types[:, None] == jnp.arange(types, dtype=jnp.int32)[None, :]).astype(F32)
    preact = [jnp.dot(elements, w_first[t], preferred_element_type=F32) for t in range(types)]
    partial = sum(
        jnp.dot(
            (jax.nn.gelu(preact[t]) * mask[:, t : t + 1]).astype(BF16),
            w_second[t],
            preferred_element_type=F32,
        )
        for t in range(types)
    )
    mlp = lax.psum_scatter(partial, "head", scatter_dimension=1, tiled=True)
    own = lax.dynamic_slice_in_dim(elements, my_columns, share, 1)
    mixed = (own.astype(F32) + mlp).astype(BF16)

    outbound = dot_nn(send_pick, mixed).astype(BF16).reshape(peers, capacity, share)
    inbound = lax.all_to_all(outbound, "det", split_axis=0, concat_axis=0, tiled=True)
    moved = dot_tn(recv_pick, inbound.reshape(peers * capacity, share)).astype(BF16)
    moved = lax.all_gather(moved, "head", axis=1, tiled=True)

    kv_weight = key_value_weight.reshape(width, 2 * HEAD_SIZE)
    queries = dot_nn(moved, w_query).astype(BF16)
    keyval = dot_nn(moved, kv_weight).astype(BF16)
    all_kv = lax.all_gather(keyval, "det", axis=0, tiled=True)
    all_kv = all_kv.reshape(-1, BLOCK_ROWS, 2 * HEAD_SIZE)
    attended, query_grad, listing = attention(
        flat_list, owners, queries, attention_cotangent, all_kv
    )
    collected = lax.all_to_all(listing, "det", split_axis=0, concat_axis=0, tiled=True)
    belongs = (wanted[None, :] == jnp.arange(blocks, dtype=jnp.int32)[:, None]).astype(BF16)
    kv_grad = dot_nn(belongs, collected.reshape(slots, -1))
    kv_grad = kv_grad.astype(BF16).reshape(row_count, 2 * HEAD_SIZE)

    partial_back = dot_nt(query_grad, w_query) + dot_nt(kv_grad, kv_weight)
    back = lax.psum_scatter(partial_back, "head", scatter_dimension=1, tiled=True).astype(BF16)
    outbound = dot_nn(recv_pick, back).astype(BF16).reshape(peers, capacity, share)
    inbound = lax.all_to_all(outbound, "det", split_axis=0, concat_axis=0, tiled=True)
    own_up = dot_tn(send_pick, inbound.reshape(peers * capacity, share)).astype(BF16)
    upstream = lax.all_gather(own_up, "head", axis=1, tiled=True)

    input_part = 0.0
    for t in range(types):
        hidden_grad = dot_nt(upstream, w_second[t]) * mask[:, t : t + 1]
        preact_grad = jax.vjp(jax.nn.gelu, preact[t])[1](hidden_grad)[0].astype(BF16)
        input_part = input_part + dot_nt(preact_grad, w_first[t])
    input_share = lax.psum_scatter(input_part, "head", scatter_dimension=1, tiled=True)
    x_grad = (own_up.astype(F32) + input_share).astype(BF16)
    return attended, x_grad


def solution(mesh):
    return jax.shard_map(
        shards,
        mesh=mesh,
        in_specs=(
            P("det", None),
            P("det"),
            P(),
            P("det", None),
            P(None, None, "head"),
            P(None, "head", None),
            P(None, "head"),
            P(None, None, "head"),
            P("det", "head"),
        ),
        out_specs=(P("det", "head"), P("det", "head")),
        check_vma=False,
    )
```

```python
import functools

import jax
import jax.numpy as jnp
from jax import lax
from jax.experimental import pallas as pl
from jax.experimental.pallas import tpu as pltpu
from jax.sharding import PartitionSpec as P

HEAD_SIZE = 64
BLOCK_ROWS = 128
LISTED_COUNT = 16
GROUP_HEADS = 4
SCALE = HEAD_SIZE ** (-0.5)

F32 = jnp.float32
BF16 = jnp.bfloat16


def dot_nn(a, b):
    return lax.dot_general(a, b, (((1,), (0,)), ((), ())), preferred_element_type=F32)


def dot_nt(a, b):
    return lax.dot_general(a, b, (((1,), (1,)), ((), ())), preferred_element_type=F32)


def dot_tn(a, b):
    return lax.dot_general(a, b, (((0,), (0,)), ((), ())), preferred_element_type=F32)


def attention_kernel(
    list_ref, place_ref, q_ref, do_ref, kv_hbm, att_ref, dq_ref, grad_ref, kv_buf, score, sems
):
    blocks = q_ref.shape[0] // BLOCK_ROWS
    rows = GROUP_HEADS * BLOCK_ROWS
    pair = 2
    steps = LISTED_COUNT // pair
    keys = pair * BLOCK_ROWS

    for b in range(blocks):

        def start(s, carry, b=b):
            slot = b * LISTED_COUNT + s
            pltpu.make_async_copy(kv_hbm.at[list_ref[slot]], kv_buf.at[slot], sems.at[b]).start()
            return carry

        lax.fori_loop(0, LISTED_COUNT, start, 0)

    def stack(ref, b):
        base = pl.multiple_of(b * BLOCK_ROWS, BLOCK_ROWS)
        tile = ref[pl.ds(base, BLOCK_ROWS), :]
        return jnp.concatenate(
            [tile[:, g * HEAD_SIZE : (g + 1) * HEAD_SIZE] for g in range(GROUP_HEADS)], axis=0
        )

    def unstack(value_t):
        parts = [
            value_t[:, g * BLOCK_ROWS : (g + 1) * BLOCK_ROWS].T for g in range(GROUP_HEADS)
        ]
        return jnp.concatenate(parts, axis=1)

    def one_block(b, carry):
        first = b * LISTED_COUNT
        pltpu.make_async_copy(
            kv_buf.at[pl.ds(first, LISTED_COUNT)], kv_buf.at[pl.ds(first, LISTED_COUNT)], sems.at[b]
        ).wait()
        q = stack(q_ref, b) * jnp.asarray(SCALE, BF16)
        do = stack(do_ref, b)
        none = jnp.zeros_like(q)
        q_pad = jnp.concatenate([q, none], axis=1)
        do_pad = jnp.concatenate([none, do], axis=1)

        def kv_at(i):
            return kv_buf[pl.ds(first + i * pair, pair)].reshape(keys, 2 * HEAD_SIZE)

        def at(i):
            return pl.ds(pl.multiple_of(i * keys, keys), keys)

        def pass_a(i, top):
            s = dot_nt(kv_at(i), q_pad)
            score[at(i), :] = s
            return jnp.maximum(top, jnp.max(s.reshape(keys // 8, 8, rows), axis=0))

        top = lax.fori_loop(0, steps, pass_a, jnp.full((8, rows), -jnp.inf, F32), unroll=2)
        top = jnp.max(top, axis=0, keepdims=True)

        def pass_b(i, carry):
            total, acc = carry
            p = jnp.exp(score[at(i), :] - top)
            score[at(i), :] = p
            total = total + jnp.sum(p.reshape(keys // 8, 8, rows), axis=0)
            acc = acc + dot_tn(kv_at(i), p.astype(BF16))
            return total, acc

        total, acc = lax.fori_loop(
            0,
            steps,
            pass_b,
            (jnp.zeros((8, rows), F32), jnp.zeros((2 * HEAD_SIZE, rows), F32)),
            unroll=2,
        )
        inverse = 1.0 / jnp.sum(total, axis=0, keepdims=True)
        out_t = acc[HEAD_SIZE:, :] * inverse
        base = pl.multiple_of(b * BLOCK_ROWS, BLOCK_ROWS)
        att_ref[pl.ds(base, BLOCK_ROWS), :] = unstack(out_t).astype(att_ref.dtype)
        delta = jnp.sum(out_t * do.astype(F32).T, axis=0, keepdims=True)
        both = jnp.concatenate([q_pad, do_pad], axis=0)

        def pass_c(i, acc):
            prob = score[at(i), :] * inverse
            kv = kv_at(i)
            dp = dot_nt(kv, do_pad)
            ds = (prob * (dp - delta)).astype(BF16)
            acc = acc + dot_tn(kv, ds)
            grads = dot_nn(jnp.concatenate([ds, prob.astype(BF16)], axis=1), both)
            grads = grads.astype(BF16)
            for k in range(pair):
                grad_ref[place_ref[first + i * pair + k]] = grads[
                    k * BLOCK_ROWS : (k + 1) * BLOCK_ROWS
                ]
            return acc

        acc = lax.fori_loop(0, steps, pass_c, jnp.zeros((2 * HEAD_SIZE, rows), F32), unroll=2)
        dq_t = acc[:HEAD_SIZE, :] * SCALE
        dq_ref[pl.ds(base, BLOCK_ROWS), :] = unstack(dq_t).astype(dq_ref.dtype)
        return carry

    lax.fori_loop(0, blocks, one_block, 0)


def attention(lists, places, q, do, kv):
    slots = lists.shape[0]
    vm = pl.BlockSpec(memory_space=pltpu.VMEM)
    sm = pl.BlockSpec(memory_space=pltpu.SMEM)
    return pl.pallas_call(
        attention_kernel,
        out_shape=(
            jax.ShapeDtypeStruct(q.shape, BF16),
            jax.ShapeDtypeStruct(q.shape, BF16),
            jax.ShapeDtypeStruct((slots, BLOCK_ROWS, 2 * HEAD_SIZE), BF16),
        ),
        in_specs=[sm, sm, vm, vm, pl.BlockSpec(memory_space=pl.ANY)],
        out_specs=(vm, vm, vm),
        scratch_shapes=[
            pltpu.VMEM((slots, BLOCK_ROWS, 2 * HEAD_SIZE), BF16),
            pltpu.VMEM((LISTED_COUNT * BLOCK_ROWS, GROUP_HEADS * BLOCK_ROWS), F32),
            pltpu.SemaphoreType.DMA((slots // LISTED_COUNT,)),
        ],
        compiler_params=pltpu.CompilerParams(vmem_limit_bytes=40 << 20),
        name="attention",
    )(lists, places, q, do, kv)


XS, ZS, CS, YS = 4, 8, 2, 4
PEERS = XS * ZS * CS
MESH = pl.DeviceIdType.MESH
Z_ORDER = (4, 3, 5, 2, 6, 1, 7, 0)
Y_ORDER = (2, 1, 3)


def push(src, dst, send_sem, recv_sem, device):
    pltpu.make_async_remote_copy(
        src_ref=src,
        dst_ref=dst,
        send_sem=send_sem,
        recv_sem=recv_sem,
        device_id=device,
        device_id_type=MESH,
    ).start()


def wait(ref, sem):
    pltpu.make_async_copy(ref, ref, sem).wait()


def place():
    me = lax.axis_index("det")
    return me, me // (ZS * CS), lax.rem(me // CS, ZS), lax.rem(me, CS), lax.axis_index("head")


def greet():
    me, _, _, _, y = place()
    sem = pltpu.get_barrier_semaphore()

    def signal(k, carry):
        peer = lax.rem(me + k, PEERS)
        pl.semaphore_signal(sem, inc=1, device_id={"det": peer}, device_id_type=MESH)
        return carry

    lax.fori_loop(1, PEERS, signal, 0)
    for k in range(1, YS):
        pl.semaphore_signal(sem, inc=1, device_id={"head": lax.rem(y + k, YS)}, device_id_type=MESH)


def greeted():
    pl.semaphore_wait(pltpu.get_barrier_semaphore(), PEERS - 1 + YS - 1)


def span(index, size):
    return pl.ds(pl.multiple_of(index * size, size), size)


def scatter_sum(part, sent, landed, send_sem, recv_sem):
    y = lax.axis_index("head")
    for i, j in enumerate(Y_ORDER):
        to = lax.rem(y + j, YS)
        sent[i] = part(to).astype(BF16)
        push(sent.at[i], landed.at[i], send_sem.at[i], recv_sem.at[i], {"head": to})
    total = part(y)
    for i in range(YS - 1):
        wait(landed.at[i], recv_sem.at[i])
        total = total + landed[i].astype(F32)
        wait(sent.at[i], send_sem.at[i])
    return total


def gather_head(ref, send_sem, recv_sem):
    y = lax.axis_index("head")
    for i, j in enumerate(Y_ORDER):
        to = lax.rem(y + j, YS)
        push(ref.at[y], ref.at[y], send_sem.at[i], recv_sem.at[i], {"head": to})


def gather_head_wait(ref, i, send_sem, recv_sem):
    y = lax.axis_index("head")
    source = lax.rem(y + YS - Y_ORDER[i], YS)
    wait(ref.at[source], recv_sem.at[i])
    wait(ref.at[source], send_sem.at[i])
    return source


def exchange(outbound, inbound, send_sem, recv_sem):
    me = lax.axis_index("det")

    def send(k, carry):
        peer = lax.rem(me + k, PEERS)
        push(outbound.at[peer], inbound.at[me], send_sem, recv_sem, {"det": peer})
        return carry

    lax.fori_loop(1, PEERS, send, 0)
    inbound[me] = outbound[me]
    wait(inbound.at[pl.ds(0, PEERS - 1)], recv_sem)
    wait(outbound.at[pl.ds(0, PEERS - 1)], send_sem)


def gather_blocks(kv, send_sem, recv_sem):
    me, x, z, c, _ = place()

    def at(jx, jz, core):
        return (lax.rem(x + jx, XS) * ZS + lax.rem(z + jz + ZS, ZS)) * CS + core

    def give(b, to):
        push(kv.at[b], kv.at[b], send_sem, recv_sem.at[b], {"det": to})

    def got(b):
        wait(kv.at[b], recv_sem.at[b])

    sister, right, left = at(0, 0, 1 - c), at(0, 1, c), at(0, -1, c)
    others = (1, 3, 2)

    @pl.when(c == 0)
    def _():
        for j in others:
            give(me, at(j, 0, c))
        for j in (0,) + others:
            b = at(j, 0, c)
            if j:
                got(b)
            give(b, right)
            give(b, left)
            give(b, sister)
        for s in range(1, 5):
            for i, j in enumerate((0,) + others):
                reach = 4 if i % 2 == 0 else 3
                for sign, last, to in ((-1, reach, right), (1, 7 - reach, left)):
                    if s <= last:
                        b = at(j, sign * s, c)
                        got(b)
                        if s < last:
                            give(b, to)
                        give(b, sister)

    @pl.when(c == 1)
    def _():
        give(me, right)
        give(me, left)
        order = [0]
        for j in others:
            give(me, at(j, 0, c))
        give(me, sister)
        for s in range(1, 5):
            for sign, last, to in ((-1, 4, right), (1, 3, left)):
                if s <= last:
                    order.append(sign * s)
                    b = at(0, sign * s, c)
                    got(b)
                    if s < last:
                        give(b, to)
                    for j in others:
                        give(b, at(j, 0, c))
                    give(b, sister)
        for s in order:
            for j in others:
                b = at(j, s, c)
                got(b)
                give(b, sister)

    def rest(i, carry):
        got(i * CS + 1 - c)
        return carry

    lax.fori_loop(0, PEERS // CS, rest, 0)
    wait(kv.at[pl.ds(0, PEERS - 1)], send_sem)


def pick_rows(column, width):
    ids = lax.broadcasted_iota(jnp.int32, (column.shape[0], width), 1)
    return jnp.where(column == ids, 1.0, 0.0).astype(BF16)


def pick_slots(row, height):
    ids = lax.broadcasted_iota(jnp.int32, (height, row.shape[1]), 0)
    return jnp.where(row == ids, 1.0, 0.0).astype(BF16)


def forward_kernel(
    x_ref, mask_ref, w1_ref, w2_ref, wq_ref, wkv_ref, send_ref, recv_ref,
    q_ref, kv_ref,
    hidden, sent, landed, outbound, inbound, moved,
    y_send, y_recv, g_send, g_recv, x_send, x_recv, kv_send, kv_recv,
):
    me, _, _, _, y = place()
    rows, width = x_ref.shape
    share = width // YS
    types, _, units = w1_ref.shape
    greet()
    step = 256
    for t in range(types):
        for k in range(units // step):
            pre = dot_nn(x_ref[...], w1_ref[t, :, k * step : (k + 1) * step])
            act = jax.nn.gelu(pre) * mask_ref[:, t : t + 1]
            hidden[:, t * units + k * step : t * units + (k + 1) * step] = act.astype(BF16)
    greeted()
    total = scatter_sum(
        lambda g: dot_nn(hidden[...], w2_ref[:, span(g, share)]), sent, landed, y_send, y_recv
    )
    mixed = (x_ref[:, span(y, share)].astype(F32) + total).astype(BF16)
    packed = dot_nn(pick_rows(send_ref[...], rows), mixed).astype(BF16)
    outbound[...] = packed.reshape(outbound.shape)
    exchange(outbound, inbound, x_send, x_recv)
    slots = inbound[...].reshape(-1, share)
    moved[y] = dot_nn(pick_slots(recv_ref[...], rows), slots).astype(BF16)
    gather_head(moved, g_send, g_recv)

    def project(g):
        m = moved[g]
        return dot_nn(m, wq_ref[span(g, share), :]), dot_nn(m, wkv_ref[span(g, share), :])

    q, kv = project(y)
    for i in range(YS - 1):
        more = project(gather_head_wait(moved, i, g_send, g_recv))
        q, kv = q + more[0], kv + more[1]
    kv_ref[me] = kv.astype(BF16)
    q_ref[...] = q.astype(BF16)
    gather_blocks(kv_ref, kv_send, kv_recv)


VM = pl.BlockSpec(memory_space=pltpu.VMEM)
SM = pl.BlockSpec(memory_space=pltpu.SMEM)
DMA = pltpu.SemaphoreType.DMA


def forward(x, mask, w1, w2, wq, wkv, send_col, recv_row):
    rows, width = x.shape
    share = width // YS
    capacity = 2 * rows // PEERS
    return pl.pallas_call(
        forward_kernel,
        out_shape=(
            jax.ShapeDtypeStruct((rows, wq.shape[1]), BF16),
            jax.ShapeDtypeStruct((PEERS, rows, wkv.shape[1]), BF16),
        ),
        in_specs=[VM] * 8,
        out_specs=(VM, VM),
        scratch_shapes=[
            pltpu.VMEM((rows, w2.shape[0]), BF16),
            pltpu.VMEM((YS - 1, rows, share), BF16),
            pltpu.VMEM((YS - 1, rows, share), BF16),
            pltpu.VMEM((PEERS, capacity, share), BF16),
            pltpu.VMEM((PEERS, capacity, share), BF16),
            pltpu.VMEM((YS, rows, share), BF16),
            DMA((YS - 1,)),
            DMA((YS - 1,)),
            DMA((YS - 1,)),
            DMA((YS - 1,)),
            DMA,
            DMA,
            DMA,
            DMA((PEERS,)),
        ],
        compiler_params=pltpu.CompilerParams(
            collective_id=1, has_side_effects=True, vmem_limit_bytes=56 << 20
        ),
        name="forward",
    )(x, mask, w1, w2, wq, wkv, send_col, recv_row)


def return_listings(
    id_ref, g_ref, id_near, near, far_out, far_in,
    id_send, id_recv, near_send, near_recv, far_send, far_recv,
):
    _, x, z, c, _ = place()
    here = x * CS + c
    group = XS * CS

    def near_peer(j):
        p = lax.rem(here + j, group)
        return p, {"det": (p // CS * ZS + z) * CS + lax.rem(p, CS)}

    for j in range(1, group):
        p, to = near_peer(j)
        push(id_ref.at[p], id_near.at[j - 1], id_send, id_recv, to)
    for i, kz in enumerate(Z_ORDER):
        row = lax.rem(z + kz, ZS)
        for j in range(1, group):
            p, to = near_peer(j)
            push(
                g_ref.at[p * ZS + row], near.at[i, j - 1], near_send, near_recv.at[i], to
            )
    blocks = far_out.shape[1]
    total = None
    wait(id_near, id_recv)
    for i, kz in enumerate(Z_ORDER):
        row = lax.rem(z + kz, ZS)
        wait(near.at[i], near_recv.at[i])
        sums = [0.0] * blocks
        for j in range(group):
            value = (near[i, j - 1] if j else g_ref[here * ZS + row]).astype(F32)
            which = id_near[j - 1, pl.ds(row, 1), :] if j else id_ref[here, pl.ds(row, 1), :]
            for k in range(blocks):
                sums[k] = sums[k] + value * jnp.where(which == k, 1.0, 0.0)
        if kz:
            for k in range(blocks):
                far_out[i, k] = sums[k].astype(BF16)
            to = (x * ZS + row) * CS + c
            push(far_out.at[i], far_in.at[i], far_send, far_recv.at[i], {"det": to})
        else:
            total = sums
    for i in range(ZS - 1):
        wait(far_in.at[i], far_recv.at[i])
        for k in range(blocks):
            total[k] = total[k] + far_in[i, k].astype(F32)
    wait(id_ref.at[pl.ds(0, group - 1)], id_send)
    wait(g_ref.at[pl.ds(0, (group - 1) * ZS)], near_send)
    wait(far_out, far_send)
    return total


def backward_kernel(
    id_ref, g_ref, dq_ref, x_ref, mask_ref, w1_ref, w2_ref, wq_ref, wkv_ref, send_ref, recv_ref,
    out_ref,
    id_near, near, far_out, far_in, kv_grad, slope, pre_grad, sent, landed, outbound, inbound, upstream,
    id_send, id_recv, near_send, near_recv, far_send, far_recv,
    y_send, y_recv, g_send, g_recv, i_send, i_recv, x_send, x_recv,
):
    _, _, _, _, y = place()
    rows, width = x_ref.shape
    share = width // YS
    types, _, units = w1_ref.shape
    greet()
    step = 256
    for t in range(types):
        for k in range(units // step):
            pre = dot_nn(x_ref[...], w1_ref[t, :, k * step : (k + 1) * step])
            ones = jnp.ones_like(pre)
            grad = jax.vjp(jax.nn.gelu, pre)[1](ones)[0] * mask_ref[:, t : t + 1]
            slope[:, t * units + k * step : t * units + (k + 1) * step] = grad
    greeted()
    total = return_listings(
        id_ref, g_ref, id_near, near, far_out, far_in,
        id_send, id_recv, near_send, near_recv, far_send, far_recv,
    )
    for k in range(len(total)):
        kv_grad[k * BLOCK_ROWS : (k + 1) * BLOCK_ROWS, :] = total[k].astype(BF16)

    def back(g):
        cols = span(g, share)
        return dot_nt(dq_ref[...], wq_ref[cols, :]) + dot_nt(kv_grad[...], wkv_ref[cols, :])

    total = scatter_sum(back, sent, landed, y_send, y_recv).astype(BF16)
    packed = dot_nn(pick_rows(recv_ref[...], rows), total).astype(BF16)
    outbound[...] = packed.reshape(outbound.shape)
    exchange(outbound, inbound, x_send, x_recv)
    slots = inbound[...].reshape(-1, share)
    upstream[y] = dot_nn(pick_slots(send_ref[...], rows), slots).astype(BF16)
    gather_head(upstream, g_send, g_recv)
    for i in range(YS - 1):
        gather_head_wait(upstream, i, g_send, g_recv)
    for k in range(types * units // step):
        cols = slice(k * step, (k + 1) * step)
        grad = 0.0
        for g in range(YS):
            grad = grad + dot_nt(upstream[g], w2_ref[cols, g * share : (g + 1) * share])
        pre_grad[:, cols] = (grad * slope[:, cols]).astype(BF16)

    def inputs(g):
        part = 0.0
        for t in range(types):
            part = part + dot_nt(
                pre_grad[:, t * units : (t + 1) * units], w1_ref[t, span(g, share), :]
            )
        return part

    total = scatter_sum(inputs, sent, landed, i_send, i_recv)
    out_ref[...] = (upstream[y].astype(F32) + total).astype(BF16)


def backward(ids, g, dq, x, mask, w1, w2, wq, wkv, send_row, recv_col):
    rows, width = x.shape
    share = width // YS
    capacity = 2 * rows // PEERS
    blocks = rows // BLOCK_ROWS
    tile = (BLOCK_ROWS, 2 * HEAD_SIZE)
    return pl.pallas_call(
        backward_kernel,
        out_shape=jax.ShapeDtypeStruct((rows, share), BF16),
        in_specs=[VM] * 11,
        out_specs=VM,
        scratch_shapes=[
            pltpu.VMEM((XS * CS - 1, ZS, 128), jnp.int32),
            pltpu.VMEM((ZS, XS * CS - 1) + tile, BF16),
            pltpu.VMEM((ZS - 1, blocks) + tile, BF16),
            pltpu.VMEM((ZS - 1, blocks) + tile, BF16),
            pltpu.VMEM((rows, 2 * HEAD_SIZE), BF16),
            pltpu.VMEM((rows, w2.shape[0]), F32),
            pltpu.VMEM((rows, w2.shape[0]), BF16),
            pltpu.VMEM((YS - 1, rows, share), BF16),
            pltpu.VMEM((YS - 1, rows, share), BF16),
            pltpu.VMEM((PEERS, capacity, share), BF16),
            pltpu.VMEM((PEERS, capacity, share), BF16),
            pltpu.VMEM((YS, rows, share), BF16),
            DMA,
            DMA,
            DMA,
            DMA((ZS,)),
            DMA,
            DMA((ZS - 1,)),
            DMA((YS - 1,)),
            DMA((YS - 1,)),
            DMA((YS - 1,)),
            DMA((YS - 1,)),
            DMA((YS - 1,)),
            DMA((YS - 1,)),
            DMA,
            DMA,
        ],
        compiler_params=pltpu.CompilerParams(
            collective_id=2, has_side_effects=True, vmem_limit_bytes=56 << 20
        ),
        name="backward",
    )(ids, g, dq, x, mask, w1, w2, wq, wkv, send_row, recv_col)


def before(counts):
    ids = jnp.arange(counts.shape[0], dtype=jnp.int32)
    earlier = ids[None, :] < ids[:, None]
    return jnp.sum(jnp.where(earlier, counts[None, :], 0), axis=1, dtype=jnp.int32)


def slot_rows(counts, capacity):
    within = jnp.arange(capacity, dtype=jnp.int32)[None, :]
    rows = jnp.where(within < counts[:, None], before(counts)[:, None] + within, -1)
    return rows.reshape(-1)


def shards(
    elements,
    element_types,
    handover_counts,
    block_lists,
    w_first,
    w_second,
    w_query,
    key_value_weight,
    attention_cotangent,
):
    me = lax.axis_index("det")
    row_count, width = elements.shape
    types, units = w_second.shape[:2]
    capacity = 2 * row_count // PEERS
    send_rows = slot_rows(
        lax.dynamic_index_in_dim(handover_counts, me, 0, keepdims=False), capacity
    )
    recv_rows = slot_rows(
        lax.dynamic_index_in_dim(handover_counts, me, 1, keepdims=False), capacity
    )

    blocks = row_count // BLOCK_ROWS
    slots = blocks * LISTED_COUNT
    flat_list = block_lists.reshape(slots)
    owners = flat_list // blocks
    places = (owners // (ZS * CS) * CS + owners % CS) * ZS + owners // CS % ZS
    ordered = jnp.sum(
        jnp.where(
            places[None, :] == jnp.arange(slots, dtype=jnp.int32)[:, None],
            (flat_list % blocks)[None, :],
            0,
        ),
        axis=1,
        dtype=jnp.int32,
    )
    ids = jnp.broadcast_to(ordered.reshape(XS * CS, ZS, 1), (XS * CS, ZS, 128))

    mask = (element_types[:, None] == jnp.arange(types, dtype=jnp.int32)[None, :]).astype(F32)
    w2 = w_second.reshape(types * units, width)
    kv_weight = key_value_weight.reshape(width, 2 * HEAD_SIZE)
    queries, all_kv = forward(
        elements, mask, w_first, w2, w_query, kv_weight, send_rows[:, None], recv_rows[None, :]
    )
    attended, query_grad, listing = attention(
        flat_list,
        places,
        queries,
        attention_cotangent,
        all_kv.reshape(-1, BLOCK_ROWS, 2 * HEAD_SIZE),
    )
    x_grad = backward(
        ids, listing, query_grad, elements, mask, w_first, w2, w_query, kv_weight,
        send_rows[None, :], recv_rows[:, None],
    )
    return attended, x_grad


def solution(mesh):
    return jax.shard_map(
        shards,
        mesh=mesh,
        in_specs=(
            P("det", None),
            P("det"),
            P(),
            P("det", None),
            P(None, None, "head"),
            P(None, "head", None),
            P(None, "head"),
            P(None, None, "head"),
            P("det", "head"),
        ),
        out_specs=(P("det", "head"), P("det", "head")),
        check_vma=False,
    )
```

```python
import functools

import jax
import jax.numpy as jnp
from jax import lax
from jax.experimental import pallas as pl
from jax.experimental.pallas import tpu as pltpu
from jax.sharding import PartitionSpec as P

HEAD_SIZE = 64
BLOCK_ROWS = 128
LISTED_COUNT = 16
GROUP_HEADS = 4
SCALE = HEAD_SIZE ** (-0.5)

F32 = jnp.float32
BF16 = jnp.bfloat16


def dot_nn(a, b):
    return lax.dot_general(a, b, (((1,), (0,)), ((), ())), preferred_element_type=F32)


def dot_nt(a, b):
    return lax.dot_general(a, b, (((1,), (1,)), ((), ())), preferred_element_type=F32)


def dot_tn(a, b):
    return lax.dot_general(a, b, (((0,), (0,)), ((), ())), preferred_element_type=F32)


XS, ZS, CS, YS = 4, 8, 2, 4
PEERS = XS * ZS * CS
MESH = pl.DeviceIdType.MESH
Z_ORDER = (4, 3, 5, 2, 6, 1, 7, 0)
Y_ORDER = (2, 1, 3)


def push(src, dst, send_sem, recv_sem, device):
    pltpu.make_async_remote_copy(
        src_ref=src,
        dst_ref=dst,
        send_sem=send_sem,
        recv_sem=recv_sem,
        device_id=device,
        device_id_type=MESH,
    ).start()


def wait(ref, sem):
    pltpu.make_async_copy(ref, ref, sem).wait()


def place():
    me = lax.axis_index("det")
    return me, me // (ZS * CS), lax.rem(me // CS, ZS), lax.rem(me, CS), lax.axis_index("head")


def greet():
    me, _, _, _, y = place()
    sem = pltpu.get_barrier_semaphore()

    def signal(k, carry):
        peer = lax.rem(me + k, PEERS)
        pl.semaphore_signal(sem, inc=1, device_id={"det": peer}, device_id_type=MESH)
        return carry

    lax.fori_loop(1, PEERS, signal, 0)
    for k in range(1, YS):
        pl.semaphore_signal(sem, inc=1, device_id={"head": lax.rem(y + k, YS)}, device_id_type=MESH)


def greeted():
    pl.semaphore_wait(pltpu.get_barrier_semaphore(), PEERS - 1 + YS - 1)


def span(index, size):
    return pl.ds(pl.multiple_of(index * size, size), size)


def upright(row):
    return jnp.broadcast_to(row.astype(F32), (8, row.shape[1])).T[:, 0:1]


def slot_rows(counts, me, capacity):
    peers = counts.shape[0]
    down = lax.broadcasted_iota(jnp.int32, counts.shape, 0)
    along = lax.broadcasted_iota(jnp.int32, counts.shape, 1)
    own = jnp.sum(jnp.where(down == me, counts, 0.0), axis=0, keepdims=True)
    start = jnp.sum(jnp.where(down < along, upright(own), 0.0), axis=0, keepdims=True)
    wide = (peers, peers * capacity)
    peer = lax.broadcasted_iota(jnp.int32, wide, 1) // capacity
    mine = jnp.where(peer == lax.broadcasted_iota(jnp.int32, wide, 0), 1.0, 0.0)

    def expand(row):
        return jnp.sum(jnp.where(mine > 0.5, upright(row), 0.0), axis=0, keepdims=True)

    within = lax.rem(lax.broadcasted_iota(jnp.int32, (1, wide[1]), 1), capacity).astype(F32)
    return jnp.where(within < expand(own), expand(start) + within, -1.0)


def pick_rows(column, width):
    ids = lax.broadcasted_iota(jnp.int32, (column.shape[0], width), 1).astype(F32)
    return jnp.where(column == ids, 1.0, 0.0).astype(BF16)


def pick_slots(row, height):
    ids = lax.broadcasted_iota(jnp.int32, (height, row.shape[1]), 0).astype(F32)
    return jnp.where(row == ids, 1.0, 0.0).astype(BF16)


HALVES = 2
WIDE = 4


def spread_start(part, sent, landed, send_sem, recv_sem):
    y = lax.axis_index("head")
    half = sent.shape[-1]
    devices = [{"head": lax.rem(y + j, YS)} for j in Y_ORDER]

    def give(h, i):
        push(sent.at[h, i], landed.at[h, i], send_sem.at[h, i], recv_sem.at[h, i], devices[i])

    for i, j in enumerate(Y_ORDER):
        value = part(lax.rem(y + j, YS)).astype(BF16)
        for h in range(HALVES):
            sent[h, i] = value[:, h * half : (h + 1) * half]
        give(0, i)
    for h in range(1, HALVES):
        for i in range(YS - 1):
            give(h, i)
    return part(y)


def spread_sum(own, h, sent, landed, send_sem, recv_sem):
    half = sent.shape[-1]
    total = own[:, h * half : (h + 1) * half]
    for i in range(YS - 1):
        wait(landed.at[h, i], recv_sem.at[h, i])
        total = total + landed[h, i].astype(F32)
        wait(sent.at[h, i], send_sem.at[h, i])
    return total


class Sum:
    def __init__(self, bufs):
        (self.far, self.far_in, self.near, self.near_in, self.hold,
         self.fs, self.fr, self.ns, self.nr) = bufs
        self.y = lax.axis_index("head")
        self.way = (lax.rem(self.y + 1, YS), lax.rem(self.y + YS - 1, YS))
        rows, self.half = self.far.shape[1:]
        self.rows = (pl.ds(0, rows // 2), pl.ds(rows // 2, rows // 2))
        self.cut = rows // 2

    def give_far(self, h, w):
        r = self.rows[w]
        push(
            self.far.at[h, r], self.far_in.at[h, r], self.fs.at[h, w], self.fr.at[h, w],
            {"head": self.way[w]},
        )

    def give_near(self, h, w, k):
        r = self.rows[k]
        push(
            self.near.at[h, w, r], self.near_in.at[h, w, r], self.ns.at[h, w, k],
            self.nr.at[h, w, k], {"head": self.way[w]},
        )

    def start(self, part):
        half = self.half
        value = part(lax.rem(self.y + 2, YS)).astype(BF16)
        for h in range(HALVES):
            self.far[h] = value[:, h * half : (h + 1) * half]
            for w in range(2):
                self.give_far(h, w)
        for w in range(2):
            value = part(self.way[w])
            mine = slice(w * self.cut, (w + 1) * self.cut)
            rest = slice((1 - w) * self.cut, (2 - w) * self.cut)
            self.hold[w] = value[mine]
            early = value[rest].astype(BF16)
            for h in range(HALVES):
                self.near[h, w, self.rows[1 - w], :] = early[:, h * half : (h + 1) * half]
                self.give_near(h, w, 1 - w)
        self.own = part(self.y)

    def relay(self, h):
        for w in range(2):
            r = self.rows[w]
            wait(self.far_in.at[h, r], self.fr.at[h, w])
            cols = slice(h * self.half, (h + 1) * self.half)
            value = self.hold[w, :, cols] + self.far_in[h, r, :].astype(F32)
            self.near[h, w, r, :] = value.astype(BF16)
            self.give_near(h, w, w)

    def finish(self, h):
        total = self.own[:, h * self.half : (h + 1) * self.half]
        for w in range(2):
            for k in (1 - w, w):
                wait(self.near_in.at[h, w, self.rows[k]], self.nr.at[h, w, k])
            total = total + self.near_in[h, w].astype(F32)
        return total

    def drain(self):
        for h in range(HALVES):
            for w in range(2):
                wait(self.far.at[h, self.rows[w]], self.fs.at[h, w])
                for k in range(2):
                    wait(self.near.at[h, w, self.rows[k]], self.ns.at[h, w, k])


def exchange_start(outbound, inbound, send_sem, recv_sem):
    me = lax.axis_index("det")

    def send(k, carry):
        peer = lax.rem(me + k, PEERS)
        push(outbound.at[peer], inbound.at[me], send_sem, recv_sem, {"det": peer})
        return carry

    lax.fori_loop(1, PEERS, send, 0)
    inbound[me] = outbound[me]


def exchange_wait(outbound, inbound, send_sem, recv_sem):
    wait(inbound.at[pl.ds(0, PEERS - 1)], recv_sem)
    wait(outbound.at[pl.ds(0, PEERS - 1)], send_sem)


def join_start(ref, send_sem, recv_sem):
    y = lax.axis_index("head")
    for i, j in enumerate(Y_ORDER):
        to = lax.rem(y + j, YS)
        push(ref.at[y], ref.at[y], send_sem.at[i], recv_sem.at[i], {"head": to})


def join_wait(ref, i, send_sem, recv_sem):
    y = lax.axis_index("head")
    source = lax.rem(y + YS - Y_ORDER[i], YS)
    wait(ref.at[source], recv_sem.at[i])
    wait(ref.at[source], send_sem.at[i])
    return source


class Handover:
    def __init__(self, bufs):
        (self.sent, self.landed, self.out, self.inb, self.full,
         self.ss, self.sr, self.es, self.er, self.js, self.jr) = bufs

    def run(self, part, finish, pack, unpack):
        rows = self.full.shape[2]
        y = lax.axis_index("head")
        own = spread_start(part, self.sent, self.landed, self.ss, self.sr)
        for h in range(HALVES):
            value = finish(spread_sum(own, h, self.sent, self.landed, self.ss, self.sr), h)
            packed = dot_nn(pack, value).astype(BF16)
            self.out[h] = packed.reshape(self.out.shape[1:])
            exchange_start(self.out.at[h], self.inb.at[h], self.es.at[h], self.er.at[h])
        for h in range(HALVES):
            exchange_wait(self.out.at[h], self.inb.at[h], self.es.at[h], self.er.at[h])
            slots = self.inb[h].reshape(-1, self.inb.shape[-1])
            self.full[h, y] = dot_nn(unpack, slots).astype(BF16)
            join_start(self.full.at[h], self.js.at[h], self.jr.at[h])

    def parts(self):
        y = lax.axis_index("head")
        for h in range(HALVES):
            yield h, y
            for i in range(YS - 1):
                yield h, join_wait(self.full.at[h], i, self.js.at[h], self.jr.at[h])


class Spread:
    def __init__(self, ref, send_sem, recv_sem):
        self.ref, self.send_sem, self.recv_sem = ref, send_sem, recv_sem
        _, self.x, self.z, self.c, _ = place()
        self.sister, self.right, self.left = (
            self.at(0, 0, 1 - self.c), self.at(0, 1, self.c), self.at(0, -1, self.c)
        )
        others = (1, 3, 2)
        self.first, second = [], []
        for j in (0,) + others:
            self.first.append((0, j, 0, (0, 1, 2) if j else (0, 1, 2, 3)))
        for s in range(1, 5):
            for i, j in enumerate((0,) + others):
                reach = 4 if i % 2 == 0 else 3
                for sign, last, way in ((-1, reach, 0), (1, 7 - reach, 1)):
                    if s <= last:
                        self.first.append((1, j, sign * s, ((way,) if s < last else ()) + (2,)))
        second.append((0, 0, 0, (0, 1, 3, 2)))
        order = [0]
        for s in range(1, 5):
            for sign, last, way in ((-1, 4, 0), (1, 3, 1)):
                if s <= last:
                    order.append(sign * s)
                    second.append((1, 0, sign * s, ((way,) if s < last else ()) + (3, 2)))
        for s in order:
            for j in others:
                second.append((1, j, s, (2,)))
        self.second = second
        self.others = others

    def at(self, jx, jz, core):
        return (lax.rem(self.x + jx, XS) * ZS + lax.rem(self.z + jz + ZS, ZS)) * CS + core

    def blocks(self, b, count=1):
        n = self.ref.shape[0] // PEERS
        return self.ref.at[pl.ds(b * n, count * n)]

    def do(self, event):
        kind, jx, jz, ways = event
        b = self.at(jx, jz, self.c)
        if kind or jx or jz:
            wait(self.blocks(b), self.recv_sem.at[b])
        for way in ways:
            if way == 3:
                targets = [self.at(j, 0, self.c) for j in self.others]
            else:
                targets = [(self.right, self.left, self.sister)[way]]
            for to in targets:
                push(
                    self.blocks(b), self.blocks(b), self.send_sem, self.recv_sem.at[b], {"det": to}
                )

    def event(self, i, when=None):
        for core, events in ((0, self.first), (1, self.second)):
            if i < len(events):
                cond = self.c == core
                if when is not None:
                    cond = jnp.logical_and(cond, when)
                pl.when(cond)(functools.partial(self.do, events[i]))

    def count(self):
        return max(len(self.first), len(self.second))

    def finish(self):
        def rest(i, carry):
            b = i * CS + 1 - self.c
            wait(self.blocks(b), self.recv_sem.at[b])
            return carry

        lax.fori_loop(0, PEERS // CS, rest, 0)
        wait(self.blocks(0, PEERS - 1), self.send_sem)


class Return:
    def __init__(self, id_ref, id_near, bufs):
        (self.g, self.near, self.far_out, self.far_in,
         self.near_send, self.near_recv, self.far_send, self.far_recv) = bufs
        self.id_ref, self.id_near = id_ref, id_near
        _, self.x, self.z, self.c, _ = place()
        self.here = self.x * CS + self.c
        self.group = XS * CS
        self.total = None

    def peer(self, j):
        p = lax.rem(self.here + j, self.group)
        return p, {"det": (p // CS * ZS + self.z) * CS + lax.rem(p, CS)}

    def start(self):
        for i, kz in enumerate(Z_ORDER):
            row = lax.rem(self.z + kz, ZS)
            for j in range(1, self.group):
                p, to = self.peer(j)
                push(
                    self.g.at[p * ZS + row], self.near.at[i, j - 1],
                    self.near_send, self.near_recv.at[i], to,
                )

    def combine(self, i):
        blocks = self.far_out.shape[1]
        row = lax.rem(self.z + Z_ORDER[i], ZS)
        wait(self.near.at[i], self.near_recv.at[i])
        sums = [0.0] * blocks
        for j in range(self.group):
            value = (self.near[i, j - 1] if j else self.g[self.here * ZS + row]).astype(F32)
            if j:
                which = self.id_near[j - 1, pl.ds(row, 1), :]
            else:
                which = self.id_ref[self.here, pl.ds(row, 1), :]
            for k in range(blocks):
                sums[k] = sums[k] + value * jnp.where(which == k, 1.0, 0.0)
        if i == ZS - 1:
            return sums
        for k in range(blocks):
            self.far_out[i, k] = sums[k].astype(BF16)
        to = (self.x * ZS + row) * CS + self.c
        push(
            self.far_out.at[i], self.far_in.at[i], self.far_send, self.far_recv.at[i], {"det": to}
        )
        return None

    def finish(self, total):
        for i in range(ZS - 1):
            wait(self.far_in.at[i], self.far_recv.at[i])
            for k in range(len(total)):
                total[k] = total[k] + self.far_in[i, k].astype(F32)
        wait(self.g.at[pl.ds(0, (self.group - 1) * ZS)], self.near_send)
        wait(self.far_out, self.far_send)
        return jnp.concatenate(total, axis=1)


def head_rows(value):
    t = value.T
    return jnp.concatenate(
        [t[g * HEAD_SIZE : (g + 1) * HEAD_SIZE] for g in range(GROUP_HEADS)], axis=1
    )


def head_columns(value):
    return jnp.concatenate(
        [value[:, g * BLOCK_ROWS : (g + 1) * BLOCK_ROWS] for g in range(GROUP_HEADS)], axis=0
    ).T


def kernel(
    list_ref, slot_ref, x_ref, kind_ref, do_ref, w1_ref, w2_ref, wq_ref, wkv_ref,
    count_ref,
    att_ref, out_ref,
    hidden, slope, pick_a, pick_b, q_t, do_t, kvt, score, prob, glist, stat, dq, kv_grad,
    id_own, id_near,
    *rest,
):
    rest = list(rest)

    def take(n):
        got = rest[:n]
        del rest[:n]
        return got

    there, back = Handover(take(11)), Handover(take(11))
    blocks_of = Spread(kvt, *take(2))
    id_send, id_recv = take(2)
    ret_v = Return(id_own, id_near, take(8))
    ret_k = Return(id_own, id_near, take(8))
    last = Sum(take(9))

    me, _, _, _, y = place()
    rows, width = x_ref.shape
    share = width // YS
    half = share // HALVES
    types, _, units = w1_ref.shape
    blocks = rows // BLOCK_ROWS
    lanes = GROUP_HEADS * BLOCK_ROWS
    greet()

    def name(p, carry):
        slot = slot_ref[p]
        which = lax.rem(list_ref[slot // LISTED_COUNT, lax.rem(slot, LISTED_COUNT)], blocks)
        id_own[p // ZS, pl.ds(lax.rem(p, ZS), 1), :] = jnp.full((1, 128), which, jnp.int32)
        return carry

    lax.fori_loop(0, XS * CS * ZS, name, 0)
    counts = count_ref[...].astype(F32)
    capacity = there.out.shape[2]
    send_row = slot_rows(counts, me, capacity)
    recv_row = slot_rows(counts.T, me, capacity)
    kinds = upright(kind_ref[...])
    step = 256
    for t in range(types):
        for k in range(units // step):
            cols = slice(t * units + k * step, t * units + (k + 1) * step)
            pre = dot_nn(x_ref[...], w1_ref[t, :, k * step : (k + 1) * step])
            keep = jnp.where(kinds == t, 1.0, 0.0)
            act, pull = jax.vjp(jax.nn.gelu, pre)
            hidden[:, cols] = (act * keep).astype(BF16)
            slope[:, cols] = pull(jnp.ones_like(pre))[0] * keep
    greeted()
    for j in range(1, XS * CS):
        p, to = ret_v.peer(j)
        push(id_own.at[p], id_near.at[j - 1], id_send, id_recv, to)
    pick_a[...] = pick_rows(upright(send_row), rows)
    pick_b[...] = pick_slots(recv_row, rows)

    def finish_there(total, h):
        own = x_ref[:, pl.ds(pl.multiple_of(y * share + h * half, half), half)]
        return (own.astype(F32) + total).astype(BF16)

    there.run(
        lambda g: dot_nn(hidden[...], w2_ref[:, span(g, share)]),
        finish_there, pick_a[...], pick_b[...],
    )
    for b in range(blocks):
        do_t[b] = head_rows(do_ref[b * BLOCK_ROWS : (b + 1) * BLOCK_ROWS, :].astype(F32)).astype(
            BF16
        )
    q, kv = 0.0, 0.0
    for h, g in there.parts():
        m = there.full[h, g]
        cols = pl.ds(pl.multiple_of(g * share + h * half, half), half)
        q = q + dot_nn(m, wq_ref[cols, :])
        kv = kv + dot_nt(wkv_ref[:, cols], m)
    kv = kv.astype(BF16)
    for b in range(blocks):
        cols = slice(b * BLOCK_ROWS, (b + 1) * BLOCK_ROWS)
        kvt[me * blocks + b] = kv[:, cols]
    for i in range(blocks_of.count()):
        blocks_of.event(i)
        if i == 0:
            q = q.astype(BF16).astype(F32) * SCALE
            for b in range(blocks):
                q_t[b] = head_rows(q[b * BLOCK_ROWS : (b + 1) * BLOCK_ROWS, :]).astype(BF16)
    blocks_of.finish()

    pieces = LISTED_COUNT // WIDE
    span_keys = WIDE * BLOCK_ROWS

    def listed(b, first, part):
        rows_of = slice(part * HEAD_SIZE, (part + 1) * HEAD_SIZE)
        return jnp.concatenate(
            [kvt[list_ref[b, first + k], rows_of, :] for k in range(WIDE)], axis=1
        )

    def soft(b, carry):
        base = b * LISTED_COUNT
        top = jnp.full((8, lanes), -jnp.inf, F32)
        for i in range(pieces):
            value = dot_tn(listed(b, i * WIDE, 0), q_t[b])
            score[i * span_keys : (i + 1) * span_keys, :] = value
            top = jnp.maximum(top, jnp.max(value.reshape(-1, 8, lanes), axis=0))
        top = jnp.max(top, axis=0, keepdims=True)
        total = jnp.zeros((8, lanes), F32)
        for i in range(pieces):
            value = jnp.exp(score[i * span_keys : (i + 1) * span_keys, :] - top)
            total = total + jnp.sum(value.reshape(-1, 8, lanes), axis=0)
            prob[b, i * span_keys : (i + 1) * span_keys, :] = value.astype(BF16)
        inverse = 1.0 / jnp.sum(total, axis=0, keepdims=True)
        stat[b] = jnp.broadcast_to(inverse, (8, lanes))
        scaled = (do_t[b].astype(F32) * inverse).astype(BF16)
        for i in range(pieces):
            grad = dot_nt(scaled, prob[b, i * span_keys : (i + 1) * span_keys, :]).astype(BF16)
            for k in range(WIDE):
                glist[base + i * WIDE + k] = grad[:, k * BLOCK_ROWS : (k + 1) * BLOCK_ROWS]
        return carry

    lax.fori_loop(0, blocks, soft, 0)

    def reorder(ref):
        def one(i, carry):
            ref[i] = glist[slot_ref[i]]
            return carry

        lax.fori_loop(0, ref.shape[0], one, 0, unroll=8)

    reorder(ret_v.g)
    ret_v.start()
    wait(id_near, id_recv)
    wait(id_own.at[pl.ds(0, XS * CS - 1)], id_send)

    def grads(b, carry):
        base = b * LISTED_COUNT
        acc = jnp.zeros((HEAD_SIZE, lanes), F32)
        for i in range(pieces):
            acc = acc + dot_nn(
                listed(b, i * WIDE, 1), prob[b, i * span_keys : (i + 1) * span_keys, :]
            )
        for k in range(1, blocks):
            pl.when(b == k)(functools.partial(ret_v.combine, k - 1))
        inverse = stat[b, 0:1, :]
        out_t = acc * inverse
        where = pl.ds(pl.multiple_of(b * BLOCK_ROWS, BLOCK_ROWS), BLOCK_ROWS)
        att_ref[where, :] = head_columns(out_t)
        d = do_t[b]
        delta = jnp.sum(out_t * d.astype(F32), axis=0, keepdims=True)
        acc = jnp.zeros((HEAD_SIZE, lanes), F32)
        for i in range(pieces):
            p = prob[b, i * span_keys : (i + 1) * span_keys, :].astype(F32) * inverse
            dp = dot_tn(listed(b, i * WIDE, 1), d)
            ds = (p * (dp - delta)).astype(BF16)
            acc = acc + dot_nn(listed(b, i * WIDE, 0), ds)
            grad = dot_nt(q_t[b], ds).astype(BF16)
            for k in range(WIDE):
                glist[base + i * WIDE + k] = grad[:, k * BLOCK_ROWS : (k + 1) * BLOCK_ROWS]
        dq[where, :] = head_columns(acc * SCALE).astype(BF16)
        return carry

    lax.fori_loop(0, blocks, grads, 0)
    reorder(ret_k.g)
    ret_k.start()
    for i in range(blocks - 1, ZS - 1):
        ret_v.combine(i)
    total = ret_v.combine(ZS - 1)
    for i in range(4):
        ret_k.combine(i)
    total = ret_v.finish(total)
    kv_grad[:, HEAD_SIZE:] = total.T.astype(BF16)
    for i in range(4, ZS - 1):
        ret_k.combine(i)
    pick_a[...] = pick_rows(upright(recv_row), rows)
    pick_b[...] = pick_slots(send_row, rows)
    total = ret_k.finish(ret_k.combine(ZS - 1))
    kv_grad[:, :HEAD_SIZE] = total.T.astype(BF16)

    def back_part(g):
        cols = span(g, share)
        return dot_nt(dq[...], wq_ref[cols, :]) + dot_nn(kv_grad[...], wkv_ref[:, cols])

    back.run(back_part, lambda total, h: total.astype(BF16), pick_a[...], pick_b[...])
    joined = list(back.parts())
    for k in range(types * units // step):
        cols = slice(k * step, (k + 1) * step)
        grad = 0.0
        for h in range(HALVES):
            for g in range(YS):
                at = g * share + h * half
                grad = grad + dot_nt(back.full[h, g], w2_ref[cols, at : at + half])
        hidden[:, cols] = (grad * slope[:, cols]).astype(BF16)

    def inputs(g):
        part = 0.0
        for t in range(types):
            part = part + dot_nt(hidden[:, t * units : (t + 1) * units], w1_ref[t, span(g, share), :])
        return part

    last.start(inputs)
    for h in range(HALVES):
        last.relay(h)
    for h in range(HALVES):
        total = last.finish(h)
        out_ref[:, h * half : (h + 1) * half] = back.full[h, y].astype(F32) + total
    last.drain()


VM = pl.BlockSpec(memory_space=pltpu.VMEM)
SM = pl.BlockSpec(memory_space=pltpu.SMEM)
DMA = pltpu.SemaphoreType.DMA


def run(lists, slots, x, kinds, do, w1, w2, wq, wkv, counts):
    rows, width = x.shape
    share = width // YS
    half = share // HALVES
    capacity = 2 * rows // PEERS
    blocks = rows // BLOCK_ROWS
    count = blocks * LISTED_COUNT
    lanes = GROUP_HEADS * BLOCK_ROWS
    tile = (HEAD_SIZE, BLOCK_ROWS)
    spread = [
        pltpu.VMEM((HALVES, YS - 1, rows, half), BF16),
        pltpu.VMEM((HALVES, YS - 1, rows, half), BF16),
    ]
    pairs = [DMA((HALVES, YS - 1)), DMA((HALVES, YS - 1))]
    handover = spread + [
        pltpu.VMEM((HALVES, PEERS, capacity, half), BF16),
        pltpu.VMEM((HALVES, PEERS, capacity, half), BF16),
        pltpu.VMEM((HALVES, YS, rows, half), BF16),
    ] + pairs + [DMA((HALVES,)), DMA((HALVES,))] + pairs
    back = [
        pltpu.VMEM((count,) + tile, BF16),
        pltpu.VMEM((ZS, XS * CS - 1) + tile, BF16),
        pltpu.VMEM((ZS - 1, blocks) + tile, BF16),
        pltpu.VMEM((ZS - 1, blocks) + tile, BF16),
        DMA,
        DMA((ZS,)),
        DMA,
        DMA((ZS - 1,)),
    ]
    return pl.pallas_call(
        kernel,
        out_shape=(
            jax.ShapeDtypeStruct((rows, share), F32),
            jax.ShapeDtypeStruct((rows, share), F32),
        ),
        in_specs=[SM, SM] + [VM] * 8,
        out_specs=(VM, VM),
        scratch_shapes=[
            pltpu.VMEM((rows, w2.shape[0]), BF16),
            pltpu.VMEM((rows, w2.shape[0]), F32),
            pltpu.VMEM((PEERS * capacity, rows), BF16),
            pltpu.VMEM((rows, PEERS * capacity), BF16),
            pltpu.VMEM((blocks, HEAD_SIZE, lanes), BF16),
            pltpu.VMEM((blocks, HEAD_SIZE, lanes), BF16),
            pltpu.VMEM((PEERS * blocks, 2 * HEAD_SIZE, BLOCK_ROWS), BF16),
            pltpu.VMEM((LISTED_COUNT * BLOCK_ROWS, lanes), F32),
            pltpu.VMEM((blocks, LISTED_COUNT * BLOCK_ROWS, lanes), BF16),
            pltpu.VMEM((count,) + tile, BF16),
            pltpu.VMEM((blocks, 8, lanes), F32),
            pltpu.VMEM((rows, share), BF16),
            pltpu.VMEM((rows, 2 * HEAD_SIZE), BF16),
            pltpu.VMEM((XS * CS, ZS, 128), jnp.int32),
            pltpu.VMEM((XS * CS - 1, ZS, 128), jnp.int32),
        ]
        + handover
        + handover
        + [DMA, DMA((PEERS,))]
        + [DMA, DMA]
        + back
        + back
        + [
            pltpu.VMEM((HALVES, rows, half), BF16),
            pltpu.VMEM((HALVES, rows, half), BF16),
            pltpu.VMEM((HALVES, 2, rows, half), BF16),
            pltpu.VMEM((HALVES, 2, rows, half), BF16),
            pltpu.VMEM((2, rows // 2, share), F32),
            DMA((HALVES, 2)),
            DMA((HALVES, 2)),
            DMA((HALVES, 2, 2)),
            DMA((HALVES, 2, 2)),
        ],
        compiler_params=pltpu.CompilerParams(
            collective_id=1, has_side_effects=True, vmem_limit_bytes=63 << 20
        ),
        name="step",
    )(
        lists, slots, x, kinds, do, w1, w2, wq, wkv, counts,
    )


def shards(
    elements,
    element_types,
    handover_counts,
    block_lists,
    w_first,
    w_second,
    w_query,
    key_value_weight,
    attention_cotangent,
):
    row_count, width = elements.shape
    types, units = w_second.shape[:2]
    blocks = row_count // BLOCK_ROWS
    slots = blocks * LISTED_COUNT
    owners = block_lists // blocks
    places = (owners // (ZS * CS) * CS + owners % CS) * ZS + owners // CS % ZS
    slot_of = jnp.sum(
        jnp.where(
            places[None] == jnp.arange(slots, dtype=jnp.int32)[:, None, None],
            jnp.arange(slots, dtype=jnp.int32).reshape(1, blocks, LISTED_COUNT),
            0,
        ),
        axis=(1, 2),
        dtype=jnp.int32,
    )
    w2 = w_second.reshape(types * units, width)
    kv_weight = key_value_weight.transpose(1, 2, 0).reshape(2 * HEAD_SIZE, width)
    attended, x_grad = run(
        block_lists, slot_of, elements, element_types[None, :], attention_cotangent, w_first, w2,
        w_query, kv_weight, handover_counts,
    )
    return attended.astype(BF16), x_grad.astype(BF16)


def solution(mesh):
    return jax.shard_map(
        shards,
        mesh=mesh,
        in_specs=(
            P("det", None),
            P("det"),
            P(),
            P("det", None),
            P(None, None, "head"),
            P(None, "head", None),
            P(None, "head"),
            P(None, None, "head"),
            P("det", "head"),
        ),
        out_specs=(P("det", "head"), P("det", "head")),
        check_vma=False,
    )
```

```python
import functools

import jax
import jax.numpy as jnp
from jax import lax
from jax.experimental import pallas as pl
from jax.experimental.pallas import tpu as pltpu
from jax.sharding import PartitionSpec as P

HEAD_SIZE = 64
BLOCK_ROWS = 128
LISTED_COUNT = 16
GROUP_HEADS = 4
SCALE = HEAD_SIZE ** (-0.5)

F32 = jnp.float32
BF16 = jnp.bfloat16


def dot_nn(a, b):
    return lax.dot_general(a, b, (((1,), (0,)), ((), ())), preferred_element_type=F32)


def dot_nt(a, b):
    return lax.dot_general(a, b, (((1,), (1,)), ((), ())), preferred_element_type=F32)


def dot_tn(a, b):
    return lax.dot_general(a, b, (((0,), (0,)), ((), ())), preferred_element_type=F32)


XS, ZS, CS, YS = 4, 8, 2, 4
PEERS = XS * ZS * CS
MESH = pl.DeviceIdType.MESH
Z_ORDER = (4, 3, 5, 2, 6, 1, 7, 0)
Y_ORDER = (2, 1, 3)


def push(src, dst, send_sem, recv_sem, device):
    pltpu.make_async_remote_copy(
        src_ref=src,
        dst_ref=dst,
        send_sem=send_sem,
        recv_sem=recv_sem,
        device_id=device,
        device_id_type=MESH,
    ).start()


def wait(ref, sem):
    pltpu.make_async_copy(ref, ref, sem).wait()


def place():
    me = lax.axis_index("det")
    return me, me // (ZS * CS), lax.rem(me // CS, ZS), lax.rem(me, CS), lax.axis_index("head")


def greet():
    me, _, _, _, y = place()
    sem = pltpu.get_barrier_semaphore()

    def signal(k, carry):
        peer = lax.rem(me + k, PEERS)
        pl.semaphore_signal(sem, inc=1, device_id={"det": peer}, device_id_type=MESH)
        return carry

    lax.fori_loop(1, PEERS, signal, 0)
    for k in range(1, YS):
        pl.semaphore_signal(sem, inc=1, device_id={"head": lax.rem(y + k, YS)}, device_id_type=MESH)


def greeted():
    pl.semaphore_wait(pltpu.get_barrier_semaphore(), PEERS - 1 + YS - 1)


def span(index, size):
    return pl.ds(pl.multiple_of(index * size, size), size)


def upright(row):
    return jnp.broadcast_to(row.astype(F32), (8, row.shape[1])).T[:, 0:1]


def slot_rows(counts, me, capacity):
    peers = counts.shape[0]
    down = lax.broadcasted_iota(jnp.int32, counts.shape, 0)
    along = lax.broadcasted_iota(jnp.int32, counts.shape, 1)
    own = jnp.sum(jnp.where(down == me, counts, 0.0), axis=0, keepdims=True)
    start = jnp.sum(jnp.where(down < along, upright(own), 0.0), axis=0, keepdims=True)
    wide = (peers, peers * capacity)
    peer = lax.broadcasted_iota(jnp.int32, wide, 1) // capacity
    mine = jnp.where(peer == lax.broadcasted_iota(jnp.int32, wide, 0), 1.0, 0.0)

    def expand(row):
        return jnp.sum(jnp.where(mine > 0.5, upright(row), 0.0), axis=0, keepdims=True)

    within = lax.rem(lax.broadcasted_iota(jnp.int32, (1, wide[1]), 1), capacity).astype(F32)
    return jnp.where(within < expand(own), expand(start) + within, -1.0)


def pick_rows(column, width):
    ids = lax.broadcasted_iota(jnp.int32, (column.shape[0], width), 1).astype(F32)
    return jnp.where(column == ids, 1.0, 0.0).astype(BF16)


def pick_slots(row, height):
    ids = lax.broadcasted_iota(jnp.int32, (height, row.shape[1]), 0).astype(F32)
    return jnp.where(row == ids, 1.0, 0.0).astype(BF16)


HALVES = 2
WIDE = 4


def spread_start(part, sent, landed, send_sem, recv_sem):
    y = lax.axis_index("head")
    half = sent.shape[-1]
    devices = [{"head": lax.rem(y + j, YS)} for j in Y_ORDER]

    def give(h, i):
        push(sent.at[h, i], landed.at[h, i], send_sem.at[h, i], recv_sem.at[h, i], devices[i])

    for i, j in enumerate(Y_ORDER):
        value = part(lax.rem(y + j, YS)).astype(BF16)
        for h in range(HALVES):
            sent[h, i] = value[:, h * half : (h + 1) * half]
        give(0, i)
    for h in range(1, HALVES):
        for i in range(YS - 1):
            give(h, i)
    return part(y)


def spread_sum(own, h, sent, landed, send_sem, recv_sem):
    half = sent.shape[-1]
    total = own[:, h * half : (h + 1) * half]
    for i in range(YS - 1):
        wait(landed.at[h, i], recv_sem.at[h, i])
        total = total + landed[h, i].astype(F32)
        wait(sent.at[h, i], send_sem.at[h, i])
    return total


class Sum:
    def __init__(self, bufs):
        (self.far, self.far_in, self.near, self.near_in, self.hold,
         self.fs, self.fr, self.ns, self.nr) = bufs
        self.y = lax.axis_index("head")
        self.way = (lax.rem(self.y + 1, YS), lax.rem(self.y + YS - 1, YS))
        rows, self.half = self.far.shape[1:]
        self.rows = (pl.ds(0, rows // 2), pl.ds(rows // 2, rows // 2))
        self.cut = rows // 2

    def give_far(self, h, w):
        r = self.rows[w]
        push(
            self.far.at[h, r], self.far_in.at[h, r], self.fs.at[h, w], self.fr.at[h, w],
            {"head": self.way[w]},
        )

    def give_near(self, h, w, k):
        r = self.rows[k]
        push(
            self.near.at[h, w, r], self.near_in.at[h, w, r], self.ns.at[h, w, k],
            self.nr.at[h, w, k], {"head": self.way[w]},
        )

    def start(self, part):
        half = self.half
        value = part(lax.rem(self.y + 2, YS)).astype(BF16)
        for h in range(HALVES):
            self.far[h] = value[:, h * half : (h + 1) * half]
            for w in range(2):
                self.give_far(h, w)
        for w in range(2):
            value = part(self.way[w])
            mine = slice(w * self.cut, (w + 1) * self.cut)
            rest = slice((1 - w) * self.cut, (2 - w) * self.cut)
            self.hold[w] = value[mine]
            early = value[rest].astype(BF16)
            for h in range(HALVES):
                self.near[h, w, self.rows[1 - w], :] = early[:, h * half : (h + 1) * half]
                self.give_near(h, w, 1 - w)
        self.own = part(self.y)

    def relay(self, h):
        for w in range(2):
            r = self.rows[w]
            wait(self.far_in.at[h, r], self.fr.at[h, w])
            cols = slice(h * self.half, (h + 1) * self.half)
            value = self.hold[w, :, cols] + self.far_in[h, r, :].astype(F32)
            self.near[h, w, r, :] = value.astype(BF16)
            self.give_near(h, w, w)

    def finish(self, h):
        total = self.own[:, h * self.half : (h + 1) * self.half]
        for w in range(2):
            for k in (1 - w, w):
                wait(self.near_in.at[h, w, self.rows[k]], self.nr.at[h, w, k])
            total = total + self.near_in[h, w].astype(F32)
        return total

    def drain(self):
        for h in range(HALVES):
            for w in range(2):
                wait(self.far.at[h, self.rows[w]], self.fs.at[h, w])
                for k in range(2):
                    wait(self.near.at[h, w, self.rows[k]], self.ns.at[h, w, k])


def exchange_start(outbound, inbound, send_sem, recv_sem):
    me = lax.axis_index("det")

    def send(k, carry):
        peer = lax.rem(me + k, PEERS)
        push(outbound.at[peer], inbound.at[me], send_sem, recv_sem, {"det": peer})
        return carry

    lax.fori_loop(1, PEERS, send, 0)
    inbound[me] = outbound[me]


def exchange_wait(outbound, inbound, send_sem, recv_sem):
    wait(inbound.at[pl.ds(0, PEERS - 1)], recv_sem)
    wait(outbound.at[pl.ds(0, PEERS - 1)], send_sem)


def join_start(ref, send_sem, recv_sem):
    y = lax.axis_index("head")
    for i, j in enumerate(Y_ORDER):
        to = lax.rem(y + j, YS)
        push(ref.at[y], ref.at[y], send_sem.at[i], recv_sem.at[i], {"head": to})


def join_wait(ref, i, send_sem, recv_sem):
    y = lax.axis_index("head")
    source = lax.rem(y + YS - Y_ORDER[i], YS)
    wait(ref.at[source], recv_sem.at[i])
    wait(ref.at[source], send_sem.at[i])
    return source


class Handover:
    def __init__(self, bufs):
        (self.sent, self.landed, self.out, self.inb, self.full,
         self.ss, self.sr, self.es, self.er, self.js, self.jr) = bufs

    def run(self, part, finish, pack, unpack, prepare=None):
        y = lax.axis_index("head")
        own = spread_start(part, self.sent, self.landed, self.ss, self.sr)
        if prepare is not None:
            prepare()
        for h in range(HALVES):
            value = finish(spread_sum(own, h, self.sent, self.landed, self.ss, self.sr), h)
            packed = dot_nn(pack[...], value).astype(BF16)
            self.out[h] = packed.reshape(self.out.shape[1:])
            exchange_start(self.out.at[h], self.inb.at[h], self.es.at[h], self.er.at[h])
        for h in range(HALVES):
            exchange_wait(self.out.at[h], self.inb.at[h], self.es.at[h], self.er.at[h])
            slots = self.inb[h].reshape(-1, self.inb.shape[-1])
            self.full[h, y] = dot_nn(unpack[...], slots).astype(BF16)
            join_start(self.full.at[h], self.js.at[h], self.jr.at[h])

    def parts(self):
        y = lax.axis_index("head")
        for h in range(HALVES):
            yield h, y
            for i in range(YS - 1):
                yield h, join_wait(self.full.at[h], i, self.js.at[h], self.jr.at[h])


class Spread:
    def __init__(self, ref, send_sem, recv_sem):
        self.ref, self.send_sem, self.recv_sem = ref, send_sem, recv_sem
        _, self.x, self.z, self.c, _ = place()
        self.sister, self.right, self.left = (
            self.at(0, 0, 1 - self.c), self.at(0, 1, self.c), self.at(0, -1, self.c)
        )
        others = (1, 3, 2)
        self.first, second = [], []
        for j in (0,) + others:
            self.first.append((0, j, 0, (0, 1, 2) if j else (0, 1, 2, 3)))
        for s in range(1, 5):
            for i, j in enumerate((0,) + others):
                reach = 4 if i % 2 == 0 else 3
                for sign, last, way in ((-1, reach, 0), (1, 7 - reach, 1)):
                    if s <= last:
                        self.first.append((1, j, sign * s, ((way,) if s < last else ()) + (2,)))
        second.append((0, 0, 0, (0, 1, 3, 2)))
        order = [0]
        for s in range(1, 5):
            for sign, last, way in ((-1, 4, 0), (1, 3, 1)):
                if s <= last:
                    order.append(sign * s)
                    second.append((1, 0, sign * s, ((way,) if s < last else ()) + (3, 2)))
        for s in order:
            for j in others:
                second.append((1, j, s, (2,)))
        self.second = second
        self.others = others

    def at(self, jx, jz, core):
        return (lax.rem(self.x + jx, XS) * ZS + lax.rem(self.z + jz + ZS, ZS)) * CS + core

    def blocks(self, b, count=1):
        n = self.ref.shape[0] // PEERS
        return self.ref.at[pl.ds(b * n, count * n)]

    def do(self, event):
        kind, jx, jz, ways = event
        b = self.at(jx, jz, self.c)
        if kind or jx or jz:
            wait(self.blocks(b), self.recv_sem.at[b])
        for way in ways:
            if way == 3:
                targets = [self.at(j, 0, self.c) for j in self.others]
            else:
                targets = [(self.right, self.left, self.sister)[way]]
            for to in targets:
                push(
                    self.blocks(b), self.blocks(b), self.send_sem, self.recv_sem.at[b], {"det": to}
                )

    def event(self, i, when=None):
        for core, events in ((0, self.first), (1, self.second)):
            if i < len(events):
                cond = self.c == core
                if when is not None:
                    cond = jnp.logical_and(cond, when)
                pl.when(cond)(functools.partial(self.do, events[i]))

    def count(self):
        return max(len(self.first), len(self.second))

    def finish(self):
        def rest(i, carry):
            b = i * CS + 1 - self.c
            wait(self.blocks(b), self.recv_sem.at[b])
            return carry

        lax.fori_loop(0, PEERS // CS, rest, 0)
        wait(self.blocks(0, PEERS - 1), self.send_sem)


class Return:
    def __init__(self, id_ref, id_near, bufs):
        (self.g, self.near, self.far_out, self.far_in,
         self.near_send, self.near_recv, self.far_send, self.far_recv) = bufs
        self.id_ref, self.id_near = id_ref, id_near
        _, self.x, self.z, self.c, _ = place()
        self.here = self.x * CS + self.c
        self.group = XS * CS
        self.total = None

    def peer(self, j):
        p = lax.rem(self.here + j, self.group)
        return p, {"det": (p // CS * ZS + self.z) * CS + lax.rem(p, CS)}

    def start(self):
        for i, kz in enumerate(Z_ORDER):
            row = lax.rem(self.z + kz, ZS)
            for j in range(1, self.group):
                p, to = self.peer(j)
                push(
                    self.g.at[p * ZS + row], self.near.at[i, j - 1],
                    self.near_send, self.near_recv.at[i], to,
                )

    def combine(self, i):
        blocks = self.far_out.shape[1]
        row = lax.rem(self.z + Z_ORDER[i], ZS)
        wait(self.near.at[i], self.near_recv.at[i])
        sums = [0.0] * blocks
        for j in range(self.group):
            value = (self.near[i, j - 1] if j else self.g[self.here * ZS + row]).astype(F32)
            if j:
                which = self.id_near[j - 1, pl.ds(row, 1), :]
            else:
                which = self.id_ref[self.here, pl.ds(row, 1), :]
            for k in range(blocks):
                sums[k] = sums[k] + value * jnp.where(which == k, 1.0, 0.0)
        if i == ZS - 1:
            return sums
        for k in range(blocks):
            self.far_out[i, k] = sums[k].astype(BF16)
        to = (self.x * ZS + row) * CS + self.c
        push(
            self.far_out.at[i], self.far_in.at[i], self.far_send, self.far_recv.at[i], {"det": to}
        )
        return None

    def finish(self, total):
        for i in range(ZS - 1):
            wait(self.far_in.at[i], self.far_recv.at[i])
            for k in range(len(total)):
                total[k] = total[k] + self.far_in[i, k].astype(F32)
        wait(self.g.at[pl.ds(0, (self.group - 1) * ZS)], self.near_send)
        wait(self.far_out, self.far_send)
        return jnp.concatenate(total, axis=1)


def head_rows(value):
    t = value.T
    return jnp.concatenate(
        [t[g * HEAD_SIZE : (g + 1) * HEAD_SIZE] for g in range(GROUP_HEADS)], axis=1
    )


def head_columns(value):
    return jnp.concatenate(
        [value[:, g * BLOCK_ROWS : (g + 1) * BLOCK_ROWS] for g in range(GROUP_HEADS)], axis=0
    ).T


def kernel(
    list_ref, slot_ref, x_in, kind_ref, do_in, w1_in, w2_in, wq_in, wkv_in,
    count_ref,
    att_ref, out_ref,
    x_ref, do_ref, w1_ref, w2_ref, wq_ref, wkv_ref, load_sem,
    hidden, slope, pick_a, pick_b, q_t, do_t, kvt, score, prob, glist, stat, dq, kv_grad,
    id_own, id_near,
    *rest,
):
    rest = list(rest)

    def take(n):
        got = rest[:n]
        del rest[:n]
        return got

    there, back = Handover(take(11)), Handover(take(11))
    blocks_of = Spread(kvt, *take(2))
    id_send, id_recv = take(2)
    ret_v = Return(id_own, id_near, take(8))
    ret_k = Return(id_own, id_near, take(8))
    last = Sum(take(9))

    me, _, _, _, y = place()
    rows, width = x_ref.shape
    share = width // YS
    half = share // HALVES
    types, _, units = w1_ref.shape
    blocks = rows // BLOCK_ROWS
    lanes = GROUP_HEADS * BLOCK_ROWS
    greet()
    loads = [
        pltpu.make_async_copy(source, target, load_sem.at[i])
        for i, (source, target) in enumerate(
            (
                (x_in, x_ref), (w1_in, w1_ref), (w2_in, w2_ref),
                (do_in, do_ref), (wq_in, wq_ref), (wkv_in, wkv_ref),
            )
        )
    ]
    for load in loads:
        load.start()

    def name(p, carry):
        slot = slot_ref[p]
        which = lax.rem(list_ref[slot // LISTED_COUNT, lax.rem(slot, LISTED_COUNT)], blocks)
        id_own[p // ZS, pl.ds(lax.rem(p, ZS), 1), :] = jnp.full((1, 128), which, jnp.int32)
        return carry

    lax.fori_loop(0, XS * CS * ZS, name, 0)
    counts = count_ref[...].astype(F32)
    capacity = there.out.shape[2]
    send_row = slot_rows(counts, me, capacity)
    recv_row = slot_rows(counts.T, me, capacity)
    kinds = upright(kind_ref[...])
    step = 256
    for load in loads[:2]:
        load.wait()
    for t in range(types):
        for k in range(units // step):
            cols = slice(t * units + k * step, t * units + (k + 1) * step)
            pre = dot_nn(x_ref[...], w1_ref[t, :, k * step : (k + 1) * step])
            keep = jnp.where(kinds == t, 1.0, 0.0)
            act, pull = jax.vjp(jax.nn.gelu, pre)
            hidden[:, cols] = (act * keep).astype(BF16)
            slope[:, cols] = pull(jnp.ones_like(pre))[0] * keep
    greeted()
    for load in loads[2:]:
        load.wait()
    for j in range(1, XS * CS):
        p, to = ret_v.peer(j)
        push(id_own.at[p], id_near.at[j - 1], id_send, id_recv, to)

    def prepare():
        pick_a[...] = pick_rows(upright(send_row), rows)
        pick_b[...] = pick_slots(recv_row, rows)

    def finish_there(total, h):
        own = x_ref[:, pl.ds(pl.multiple_of(y * share + h * half, half), half)]
        return (own.astype(F32) + total).astype(BF16)

    there.run(
        lambda g: dot_nn(hidden[...], w2_ref[:, span(g, share)]),
        finish_there, pick_a, pick_b, prepare,
    )
    for b in range(blocks):
        do_t[b] = head_rows(do_ref[b * BLOCK_ROWS : (b + 1) * BLOCK_ROWS, :].astype(F32)).astype(
            BF16
        )
    q, kv = 0.0, 0.0
    for h, g in there.parts():
        m = there.full[h, g]
        cols = pl.ds(pl.multiple_of(g * share + h * half, half), half)
        q = q + dot_nn(m, wq_ref[cols, :])
        kv = kv + dot_nt(wkv_ref[:, cols], m)
    kv = kv.astype(BF16)
    for b in range(blocks):
        cols = slice(b * BLOCK_ROWS, (b + 1) * BLOCK_ROWS)
        kvt[me * blocks + b] = kv[:, cols]
    for i in range(blocks_of.count()):
        blocks_of.event(i)
        if i == 0:
            q = q.astype(BF16).astype(F32) * SCALE
            for b in range(blocks):
                q_t[b] = head_rows(q[b * BLOCK_ROWS : (b + 1) * BLOCK_ROWS, :]).astype(BF16)
    blocks_of.finish()

    pieces = LISTED_COUNT // WIDE
    span_keys = WIDE * BLOCK_ROWS

    def listed(b, first, part):
        rows_of = slice(part * HEAD_SIZE, (part + 1) * HEAD_SIZE)
        return jnp.concatenate(
            [kvt[list_ref[b, first + k], rows_of, :] for k in range(WIDE)], axis=1
        )

    def soft(b, carry):
        base = b * LISTED_COUNT
        top = jnp.full((8, lanes), -jnp.inf, F32)
        for i in range(pieces):
            value = dot_tn(listed(b, i * WIDE, 0), q_t[b])
            score[i * span_keys : (i + 1) * span_keys, :] = value
            top = jnp.maximum(top, jnp.max(value.reshape(-1, 8, lanes), axis=0))
        top = jnp.max(top, axis=0, keepdims=True)
        total = jnp.zeros((8, lanes), F32)
        for i in range(pieces):
            value = jnp.exp(score[i * span_keys : (i + 1) * span_keys, :] - top)
            total = total + jnp.sum(value.reshape(-1, 8, lanes), axis=0)
            prob[b, i * span_keys : (i + 1) * span_keys, :] = value.astype(BF16)
        inverse = 1.0 / jnp.sum(total, axis=0, keepdims=True)
        stat[b] = jnp.broadcast_to(inverse, (8, lanes))
        scaled = (do_t[b].astype(F32) * inverse).astype(BF16)
        for i in range(pieces):
            grad = dot_nt(scaled, prob[b, i * span_keys : (i + 1) * span_keys, :]).astype(BF16)
            for k in range(WIDE):
                glist[base + i * WIDE + k] = grad[:, k * BLOCK_ROWS : (k + 1) * BLOCK_ROWS]
        return carry

    lax.fori_loop(0, blocks, soft, 0)

    def reorder(ref):
        def one(i, carry):
            ref[i] = glist[slot_ref[i]]
            return carry

        lax.fori_loop(0, ref.shape[0], one, 0, unroll=8)

    reorder(ret_v.g)
    ret_v.start()
    wait(id_near, id_recv)
    wait(id_own.at[pl.ds(0, XS * CS - 1)], id_send)

    def grads(b, carry):
        base = b * LISTED_COUNT
        acc = jnp.zeros((HEAD_SIZE, lanes), F32)
        for i in range(pieces):
            acc = acc + dot_nn(
                listed(b, i * WIDE, 1), prob[b, i * span_keys : (i + 1) * span_keys, :]
            )
        for k in range(1, blocks):
            pl.when(b == k)(functools.partial(ret_v.combine, k - 1))
        inverse = stat[b, 0:1, :]
        out_t = acc * inverse
        where = pl.ds(pl.multiple_of(b * BLOCK_ROWS, BLOCK_ROWS), BLOCK_ROWS)
        att_ref[where, :] = head_columns(out_t).astype(BF16)
        d = do_t[b]
        delta = jnp.sum(out_t * d.astype(F32), axis=0, keepdims=True)
        acc = jnp.zeros((HEAD_SIZE, lanes), F32)
        for i in range(pieces):
            p = prob[b, i * span_keys : (i + 1) * span_keys, :].astype(F32) * inverse
            dp = dot_tn(listed(b, i * WIDE, 1), d)
            ds = (p * (dp - delta)).astype(BF16)
            acc = acc + dot_nn(listed(b, i * WIDE, 0), ds)
            grad = dot_nt(q_t[b], ds).astype(BF16)
            for k in range(WIDE):
                glist[base + i * WIDE + k] = grad[:, k * BLOCK_ROWS : (k + 1) * BLOCK_ROWS]
        dq[where, :] = head_columns(acc * SCALE).astype(BF16)
        return carry

    lax.fori_loop(0, blocks, grads, 0)
    reorder(ret_k.g)
    ret_k.start()
    for i in range(blocks - 1, ZS - 1):
        ret_v.combine(i)
    total = ret_v.combine(ZS - 1)
    for i in range(4):
        ret_k.combine(i)
    total = ret_v.finish(total)
    kv_grad[:, HEAD_SIZE:] = total.T.astype(BF16)
    for i in range(4, ZS - 1):
        ret_k.combine(i)
    pick_a[...] = pick_rows(upright(recv_row), rows)
    pick_b[...] = pick_slots(send_row, rows)
    total = ret_k.finish(ret_k.combine(ZS - 1))
    kv_grad[:, :HEAD_SIZE] = total.T.astype(BF16)

    def back_part(g):
        cols = span(g, share)
        return dot_nt(dq[...], wq_ref[cols, :]) + dot_nn(kv_grad[...], wkv_ref[:, cols])

    back.run(back_part, lambda total, h: total.astype(BF16), pick_a, pick_b)
    seen = 0
    for h, g in back.parts():
        seen += 1
        if seen < (h + 1) * YS:
            continue
        for k in range(types * units // step):
            cols = slice(k * step, (k + 1) * step)
            kept = (
                slice(k // 2 * rows, (k // 2 + 1) * rows), slice(k % 2 * step, (k % 2 + 1) * step)
            )
            grad = score[kept] if h else 0.0
            for group in range(YS):
                at = group * share + h * half
                grad = grad + dot_nt(back.full[h, group], w2_ref[cols, at : at + half])
            if h + 1 < HALVES:
                score[kept] = grad
            else:
                hidden[:, cols] = (grad * slope[:, cols]).astype(BF16)

    def inputs(g):
        part = 0.0
        for t in range(types):
            part = part + dot_nt(hidden[:, t * units : (t + 1) * units], w1_ref[t, span(g, share), :])
        return part

    last.start(inputs)
    for h in range(HALVES):
        last.relay(h)
    for h in range(HALVES):
        total = last.finish(h)
        value = back.full[h, y].astype(F32) + total
        out_ref[:, h * half : (h + 1) * half] = value.astype(BF16)
    last.drain()


VM = pl.BlockSpec(memory_space=pltpu.VMEM)
SM = pl.BlockSpec(memory_space=pltpu.SMEM)
HB = pl.BlockSpec(memory_space=pl.ANY)
DMA = pltpu.SemaphoreType.DMA


def run(lists, slots, x, kinds, do, w1, w2, wq, wkv, counts):
    rows, width = x.shape
    share = width // YS
    half = share // HALVES
    capacity = 2 * rows // PEERS
    blocks = rows // BLOCK_ROWS
    count = blocks * LISTED_COUNT
    lanes = GROUP_HEADS * BLOCK_ROWS
    tile = (HEAD_SIZE, BLOCK_ROWS)
    spread = [
        pltpu.VMEM((HALVES, YS - 1, rows, half), BF16),
        pltpu.VMEM((HALVES, YS - 1, rows, half), BF16),
    ]
    pairs = [DMA((HALVES, YS - 1)), DMA((HALVES, YS - 1))]
    handover = spread + [
        pltpu.VMEM((HALVES, PEERS, capacity, half), BF16),
        pltpu.VMEM((HALVES, PEERS, capacity, half), BF16),
        pltpu.VMEM((HALVES, YS, rows, half), BF16),
    ] + pairs + [DMA((HALVES,)), DMA((HALVES,))] + pairs
    back = [
        pltpu.VMEM((count,) + tile, BF16),
        pltpu.VMEM((ZS, XS * CS - 1) + tile, BF16),
        pltpu.VMEM((ZS - 1, blocks) + tile, BF16),
        pltpu.VMEM((ZS - 1, blocks) + tile, BF16),
        DMA,
        DMA((ZS,)),
        DMA,
        DMA((ZS - 1,)),
    ]
    return pl.pallas_call(
        kernel,
        out_shape=(
            jax.ShapeDtypeStruct((rows, share), BF16),
            jax.ShapeDtypeStruct((rows, share), BF16),
        ),
        in_specs=[SM, SM, HB, VM] + [HB] * 5 + [VM],
        out_specs=(VM, VM),
        scratch_shapes=[pltpu.VMEM(v.shape, BF16) for v in (x, do, w1, w2, wq, wkv)]
        + [
            DMA((6,)),
            pltpu.VMEM((rows, w2.shape[0]), BF16),
            pltpu.VMEM((rows, w2.shape[0]), F32),
            pltpu.VMEM((PEERS * capacity, rows), BF16),
            pltpu.VMEM((rows, PEERS * capacity), BF16),
            pltpu.VMEM((blocks, HEAD_SIZE, lanes), BF16),
            pltpu.VMEM((blocks, HEAD_SIZE, lanes), BF16),
            pltpu.VMEM((PEERS * blocks, 2 * HEAD_SIZE, BLOCK_ROWS), BF16),
            pltpu.VMEM((LISTED_COUNT * BLOCK_ROWS, lanes), F32),
            pltpu.VMEM((blocks, LISTED_COUNT * BLOCK_ROWS, lanes), BF16),
            pltpu.VMEM((count,) + tile, BF16),
            pltpu.VMEM((blocks, 8, lanes), F32),
            pltpu.VMEM((rows, share), BF16),
            pltpu.VMEM((rows, 2 * HEAD_SIZE), BF16),
            pltpu.VMEM((XS * CS, ZS, 128), jnp.int32),
            pltpu.VMEM((XS * CS - 1, ZS, 128), jnp.int32),
        ]
        + handover
        + handover
        + [DMA, DMA((PEERS,))]
        + [DMA, DMA]
        + back
        + back
        + [
            pltpu.VMEM((HALVES, rows, half), BF16),
            pltpu.VMEM((HALVES, rows, half), BF16),
            pltpu.VMEM((HALVES, 2, rows, half), BF16),
            pltpu.VMEM((HALVES, 2, rows, half), BF16),
            pltpu.VMEM((2, rows // 2, share), F32),
            DMA((HALVES, 2)),
            DMA((HALVES, 2)),
            DMA((HALVES, 2, 2)),
            DMA((HALVES, 2, 2)),
        ],
        compiler_params=pltpu.CompilerParams(
            collective_id=1, has_side_effects=True, vmem_limit_bytes=63 << 20
        ),
        name="step",
    )(
        lists, slots, x, kinds, do, w1, w2, wq, wkv, counts,
    )


def deliver_kernel(a_ref, b_ref, a_out, b_out):
    a_out[...] = a_ref[...]
    b_out[...] = b_ref[...]


def deliver(a, b):
    return pl.pallas_call(
        deliver_kernel,
        out_shape=tuple(jax.ShapeDtypeStruct(v.shape, v.dtype) for v in (a, b)),
        in_specs=[VM, VM],
        out_specs=(VM, VM),
        name="deliver",
    )(a, b)


def shards(
    elements,
    element_types,
    handover_counts,
    block_lists,
    w_first,
    w_second,
    w_query,
    key_value_weight,
    attention_cotangent,
):
    row_count, width = elements.shape
    types, units = w_second.shape[:2]
    blocks = row_count // BLOCK_ROWS
    slots = blocks * LISTED_COUNT
    owners = block_lists // blocks
    places = (owners // (ZS * CS) * CS + owners % CS) * ZS + owners // CS % ZS
    slot_of = jnp.sum(
        jnp.where(
            places[None] == jnp.arange(slots, dtype=jnp.int32)[:, None, None],
            jnp.arange(slots, dtype=jnp.int32).reshape(1, blocks, LISTED_COUNT),
            0,
        ),
        axis=(1, 2),
        dtype=jnp.int32,
    )
    w2 = w_second.reshape(types * units, width)
    kv_weight = key_value_weight.transpose(1, 2, 0).reshape(2 * HEAD_SIZE, width)
    attended, x_grad = run(
        block_lists, slot_of, elements, element_types[None, :], attention_cotangent, w_first, w2,
        w_query, kv_weight, handover_counts,
    )
    return deliver(attended, x_grad)


def solution(mesh):
    return jax.shard_map(
        shards,
        mesh=mesh,
        in_specs=(
            P("det", None),
            P("det"),
            P(),
            P("det", None),
            P(None, None, "head"),
            P(None, "head", None),
            P(None, "head"),
            P(None, None, "head"),
            P("det", "head"),
        ),
        out_specs=(P("det", "head"), P("det", "head")),
        check_vma=False,
    )
```

```python
import functools

import jax
import jax.numpy as jnp
from jax import lax
from jax.experimental import pallas as pl
from jax.experimental.pallas import tpu as pltpu
from jax.sharding import PartitionSpec as P

HEAD_SIZE = 64
BLOCK_ROWS = 128
LISTED_COUNT = 16
GROUP_HEADS = 4
SCALE = HEAD_SIZE ** (-0.5)

F32 = jnp.float32
BF16 = jnp.bfloat16


def dot_nn(a, b):
    return lax.dot_general(a, b, (((1,), (0,)), ((), ())), preferred_element_type=F32)


def dot_nt(a, b):
    return lax.dot_general(a, b, (((1,), (1,)), ((), ())), preferred_element_type=F32)


def dot_tn(a, b):
    return lax.dot_general(a, b, (((0,), (0,)), ((), ())), preferred_element_type=F32)


XS, ZS, CS, YS = 4, 8, 2, 4
PEERS = XS * ZS * CS
MESH = pl.DeviceIdType.MESH
Z_ORDER = (4, 3, 5, 2, 6, 1, 7, 0)
Y_ORDER = (2, 1, 3)


def push(src, dst, send_sem, recv_sem, device):
    pltpu.make_async_remote_copy(
        src_ref=src,
        dst_ref=dst,
        send_sem=send_sem,
        recv_sem=recv_sem,
        device_id=device,
        device_id_type=MESH,
    ).start()


def wait(ref, sem):
    pltpu.make_async_copy(ref, ref, sem).wait()


def place():
    me = lax.axis_index("det")
    return me, me // (ZS * CS), lax.rem(me // CS, ZS), lax.rem(me, CS), lax.axis_index("head")


def greet():
    me, _, _, _, y = place()
    sem = pltpu.get_barrier_semaphore()

    def signal(k, carry):
        peer = lax.rem(me + k, PEERS)
        pl.semaphore_signal(sem, inc=1, device_id={"det": peer}, device_id_type=MESH)
        return carry

    lax.fori_loop(1, PEERS, signal, 0)
    for k in range(1, YS):
        pl.semaphore_signal(sem, inc=1, device_id={"head": lax.rem(y + k, YS)}, device_id_type=MESH)


def greeted():
    pl.semaphore_wait(pltpu.get_barrier_semaphore(), PEERS - 1 + YS - 1)


def span(index, size):
    return pl.ds(pl.multiple_of(index * size, size), size)


def upright(row):
    return jnp.broadcast_to(row.astype(F32), (8, row.shape[1])).T[:, 0:1]


def slot_rows(counts, me, capacity):
    peers = counts.shape[0]
    down = lax.broadcasted_iota(jnp.int32, counts.shape, 0)
    along = lax.broadcasted_iota(jnp.int32, counts.shape, 1)
    own = jnp.sum(jnp.where(down == me, counts, 0.0), axis=0, keepdims=True)
    start = jnp.sum(jnp.where(down < along, upright(own), 0.0), axis=0, keepdims=True)
    wide = (peers, peers * capacity)
    peer = lax.broadcasted_iota(jnp.int32, wide, 1) // capacity
    mine = jnp.where(peer == lax.broadcasted_iota(jnp.int32, wide, 0), 1.0, 0.0)

    def expand(row):
        return jnp.sum(jnp.where(mine > 0.5, upright(row), 0.0), axis=0, keepdims=True)

    within = lax.rem(lax.broadcasted_iota(jnp.int32, (1, wide[1]), 1), capacity).astype(F32)
    return jnp.where(within < expand(own), expand(start) + within, -1.0)


def pick_rows(column, width):
    ids = lax.broadcasted_iota(jnp.int32, (column.shape[0], width), 1).astype(F32)
    return jnp.where(column == ids, 1.0, 0.0).astype(BF16)


def pick_slots(row, height):
    ids = lax.broadcasted_iota(jnp.int32, (height, row.shape[1]), 0).astype(F32)
    return jnp.where(row == ids, 1.0, 0.0).astype(BF16)


HALVES = 2
WIDE = 4


def spread_start(part, sent, landed, send_sem, recv_sem):
    y = lax.axis_index("head")
    half = sent.shape[-1]
    devices = [{"head": lax.rem(y + j, YS)} for j in Y_ORDER]

    def give(h, i):
        push(sent.at[h, i], landed.at[h, i], send_sem.at[h, i], recv_sem.at[h, i], devices[i])

    for i, j in enumerate(Y_ORDER):
        value = part(lax.rem(y + j, YS)).astype(BF16)
        for h in range(HALVES):
            sent[h, i] = value[:, h * half : (h + 1) * half]
        give(0, i)
    for h in range(1, HALVES):
        for i in range(YS - 1):
            give(h, i)
    return part(y)


def spread_sum(own, h, sent, landed, send_sem, recv_sem):
    half = sent.shape[-1]
    total = own[:, h * half : (h + 1) * half]
    for i in range(YS - 1):
        wait(landed.at[h, i], recv_sem.at[h, i])
        total = total + landed[h, i].astype(F32)
        wait(sent.at[h, i], send_sem.at[h, i])
    return total


class Sum:
    def __init__(self, bufs):
        (self.far, self.far_in, self.near, self.near_in, self.hold,
         self.fs, self.fr, self.ns, self.nr) = bufs
        self.y = lax.axis_index("head")
        self.way = (lax.rem(self.y + 1, YS), lax.rem(self.y + YS - 1, YS))
        rows, self.half = self.far.shape[1:]
        self.rows = (pl.ds(0, rows // 2), pl.ds(rows // 2, rows // 2))
        self.cut = rows // 2

    def give_far(self, h, w):
        r = self.rows[w]
        push(
            self.far.at[h, r], self.far_in.at[h, r], self.fs.at[h, w], self.fr.at[h, w],
            {"head": self.way[w]},
        )

    def give_near(self, h, w, k):
        r = self.rows[k]
        push(
            self.near.at[h, w, r], self.near_in.at[h, w, r], self.ns.at[h, w, k],
            self.nr.at[h, w, k], {"head": self.way[w]},
        )

    def start(self, part):
        half = self.half
        value = part(lax.rem(self.y + 2, YS)).astype(BF16)
        for h in range(HALVES):
            self.far[h] = value[:, h * half : (h + 1) * half]
            for w in range(2):
                self.give_far(h, w)
        for w in range(2):
            value = part(self.way[w])
            mine = slice(w * self.cut, (w + 1) * self.cut)
            rest = slice((1 - w) * self.cut, (2 - w) * self.cut)
            self.hold[w] = value[mine]
            early = value[rest].astype(BF16)
            for h in range(HALVES):
                self.near[h, w, self.rows[1 - w], :] = early[:, h * half : (h + 1) * half]
                self.give_near(h, w, 1 - w)
        self.own = part(self.y)

    def relay(self, h):
        for w in range(2):
            r = self.rows[w]
            wait(self.far_in.at[h, r], self.fr.at[h, w])
            cols = slice(h * self.half, (h + 1) * self.half)
            value = self.hold[w, :, cols] + self.far_in[h, r, :].astype(F32)
            self.near[h, w, r, :] = value.astype(BF16)
            self.give_near(h, w, w)

    def finish(self, h):
        total = self.own[:, h * self.half : (h + 1) * self.half]
        for w in range(2):
            for k in (1 - w, w):
                wait(self.near_in.at[h, w, self.rows[k]], self.nr.at[h, w, k])
            total = total + self.near_in[h, w].astype(F32)
        return total

    def drain(self):
        for h in range(HALVES):
            for w in range(2):
                wait(self.far.at[h, self.rows[w]], self.fs.at[h, w])
                for k in range(2):
                    wait(self.near.at[h, w, self.rows[k]], self.ns.at[h, w, k])


def exchange_start(outbound, inbound, send_sem, recv_sem):
    me = lax.axis_index("det")

    def send(k, carry):
        peer = lax.rem(me + k, PEERS)
        push(outbound.at[peer], inbound.at[me], send_sem, recv_sem, {"det": peer})
        return carry

    lax.fori_loop(1, PEERS, send, 0)
    inbound[me] = outbound[me]


def exchange_wait(outbound, inbound, send_sem, recv_sem):
    wait(inbound.at[pl.ds(0, PEERS - 1)], recv_sem)
    wait(outbound.at[pl.ds(0, PEERS - 1)], send_sem)


def join_start(ref, send_sem, recv_sem):
    y = lax.axis_index("head")
    for i, j in enumerate(Y_ORDER):
        to = lax.rem(y + j, YS)
        push(ref.at[y], ref.at[y], send_sem.at[i], recv_sem.at[i], {"head": to})


def join_wait(ref, i, send_sem, recv_sem):
    y = lax.axis_index("head")
    source = lax.rem(y + YS - Y_ORDER[i], YS)
    wait(ref.at[source], recv_sem.at[i])
    wait(ref.at[source], send_sem.at[i])
    return source


class Handover:
    def __init__(self, bufs):
        (self.sent, self.landed, self.out, self.inb, self.full,
         self.ss, self.sr, self.es, self.er, self.js, self.jr) = bufs

    def run(self, part, finish, pack, unpack, prepare=None):
        y = lax.axis_index("head")
        own = spread_start(part, self.sent, self.landed, self.ss, self.sr)
        if prepare is not None:
            prepare()
        for h in range(HALVES):
            value = finish(spread_sum(own, h, self.sent, self.landed, self.ss, self.sr), h)
            packed = dot_nn(pack[...], value).astype(BF16)
            self.out[h] = packed.reshape(self.out.shape[1:])
            exchange_start(self.out.at[h], self.inb.at[h], self.es.at[h], self.er.at[h])
        for h in range(HALVES):
            exchange_wait(self.out.at[h], self.inb.at[h], self.es.at[h], self.er.at[h])
            slots = self.inb[h].reshape(-1, self.inb.shape[-1])
            self.full[h, y] = dot_nn(unpack[...], slots).astype(BF16)
            join_start(self.full.at[h], self.js.at[h], self.jr.at[h])

    def parts(self):
        y = lax.axis_index("head")
        for h in range(HALVES):
            yield h, y
            for i in range(YS - 1):
                yield h, join_wait(self.full.at[h], i, self.js.at[h], self.jr.at[h])


class Spread:
    def __init__(self, ref, send_sem, recv_sem):
        self.ref, self.send_sem, self.recv_sem = ref, send_sem, recv_sem
        _, self.x, self.z, self.c, _ = place()
        self.sister, self.right, self.left = (
            self.at(0, 0, 1 - self.c), self.at(0, 1, self.c), self.at(0, -1, self.c)
        )
        others = (1, 3, 2)
        self.first, second = [], []
        for j in (0,) + others:
            self.first.append((0, j, 0, (0, 1, 2) if j else (0, 1, 2, 3)))
        for s in range(1, 5):
            for i, j in enumerate((0,) + others):
                reach = 4 if i % 2 == 0 else 3
                for sign, last, way in ((-1, reach, 0), (1, 7 - reach, 1)):
                    if s <= last:
                        self.first.append((1, j, sign * s, ((way,) if s < last else ()) + (2,)))
        second.append((0, 0, 0, (0, 1, 3, 2)))
        order = [0]
        for s in range(1, 5):
            for sign, last, way in ((-1, 4, 0), (1, 3, 1)):
                if s <= last:
                    order.append(sign * s)
                    second.append((1, 0, sign * s, ((way,) if s < last else ()) + (3, 2)))
        for s in order:
            for j in others:
                second.append((1, j, s, (2,)))
        self.second = second
        self.others = others

    def at(self, jx, jz, core):
        return (lax.rem(self.x + jx, XS) * ZS + lax.rem(self.z + jz + ZS, ZS)) * CS + core

    def blocks(self, b, count=1):
        n = self.ref.shape[0] // PEERS
        return self.ref.at[pl.ds(b * n, count * n)]

    def do(self, event):
        kind, jx, jz, ways = event
        b = self.at(jx, jz, self.c)
        if kind or jx or jz:
            wait(self.blocks(b), self.recv_sem.at[b])
        for way in ways:
            if way == 3:
                targets = [self.at(j, 0, self.c) for j in self.others]
            else:
                targets = [(self.right, self.left, self.sister)[way]]
            for to in targets:
                push(
                    self.blocks(b), self.blocks(b), self.send_sem, self.recv_sem.at[b], {"det": to}
                )

    def event(self, i, when=None):
        for core, events in ((0, self.first), (1, self.second)):
            if i < len(events):
                cond = self.c == core
                if when is not None:
                    cond = jnp.logical_and(cond, when)
                pl.when(cond)(functools.partial(self.do, events[i]))

    def count(self):
        return max(len(self.first), len(self.second))

    def finish(self):
        def rest(i, carry):
            b = i * CS + 1 - self.c
            wait(self.blocks(b), self.recv_sem.at[b])
            return carry

        lax.fori_loop(0, PEERS // CS, rest, 0)
        wait(self.blocks(0, PEERS - 1), self.send_sem)


class Return:
    def __init__(self, id_ref, id_near, bufs):
        (self.g, self.near, self.far_out, self.far_in,
         self.near_send, self.near_recv, self.far_send, self.far_recv) = bufs
        self.id_ref, self.id_near = id_ref, id_near
        _, self.x, self.z, self.c, _ = place()
        self.here = self.x * CS + self.c
        self.group = XS * CS
        self.total = None

    def peer(self, j):
        p = lax.rem(self.here + j, self.group)
        return p, {"det": (p // CS * ZS + self.z) * CS + lax.rem(p, CS)}

    def start(self):
        for i, kz in enumerate(Z_ORDER):
            row = lax.rem(self.z + kz, ZS)
            for j in range(1, self.group):
                p, to = self.peer(j)
                push(
                    self.g.at[p * ZS + row], self.near.at[i, j - 1],
                    self.near_send, self.near_recv.at[i], to,
                )

    def combine(self, i):
        blocks = self.far_out.shape[1]
        row = lax.rem(self.z + Z_ORDER[i], ZS)
        wait(self.near.at[i], self.near_recv.at[i])
        sums = [0.0] * blocks
        for j in range(self.group):
            value = (self.near[i, j - 1] if j else self.g[self.here * ZS + row]).astype(F32)
            if j:
                which = self.id_near[j - 1, pl.ds(row, 1), :]
            else:
                which = self.id_ref[self.here, pl.ds(row, 1), :]
            for k in range(blocks):
                sums[k] = sums[k] + value * jnp.where(which == k, 1.0, 0.0)
        if i == ZS - 1:
            return sums
        for k in range(blocks):
            self.far_out[i, k] = sums[k].astype(BF16)
        to = (self.x * ZS + row) * CS + self.c
        push(
            self.far_out.at[i], self.far_in.at[i], self.far_send, self.far_recv.at[i], {"det": to}
        )
        return None

    def finish(self, total):
        for i in range(ZS - 1):
            wait(self.far_in.at[i], self.far_recv.at[i])
            for k in range(len(total)):
                total[k] = total[k] + self.far_in[i, k].astype(F32)
        wait(self.g.at[pl.ds(0, (self.group - 1) * ZS)], self.near_send)
        wait(self.far_out, self.far_send)
        return jnp.concatenate(total, axis=1)


def head_rows(value):
    t = value.T
    return jnp.concatenate(
        [t[g * HEAD_SIZE : (g + 1) * HEAD_SIZE] for g in range(GROUP_HEADS)], axis=1
    )


def head_columns(value):
    return jnp.concatenate(
        [value[:, g * BLOCK_ROWS : (g + 1) * BLOCK_ROWS] for g in range(GROUP_HEADS)], axis=0
    ).T


def kernel(
    list_ref, slot_ref, x_in, kind_ref, do_in, w1_in, w2_in, wq_in, wkv_in,
    count_ref,
    att_ref, out_ref,
    x_ref, do_ref, w1_ref, w2_ref, wq_ref, wkv_ref, load_sem,
    hidden, slope, pick_a, pick_b, q_t, do_t, kvt, score, prob, glist, stat, dq, kv_grad,
    id_own, id_near,
    *rest,
):
    rest = list(rest)

    def take(n):
        got = rest[:n]
        del rest[:n]
        return got

    there, back = Handover(take(11)), Handover(take(11))
    blocks_of = Spread(kvt, *take(2))
    id_send, id_recv = take(2)
    ret_v = Return(id_own, id_near, take(8))
    ret_k = Return(id_own, id_near, take(8))
    last = Sum(take(9))

    me, _, _, _, y = place()
    rows, width = x_ref.shape
    share = width // YS
    half = share // HALVES
    types, _, units = w1_ref.shape
    blocks = rows // BLOCK_ROWS
    lanes = GROUP_HEADS * BLOCK_ROWS
    greet()
    loads = [
        pltpu.make_async_copy(source, target, load_sem.at[i])
        for i, (source, target) in enumerate(
            (
                (x_in, x_ref), (w1_in, w1_ref), (w2_in, w2_ref),
                (do_in, do_ref), (wq_in, wq_ref), (wkv_in, wkv_ref),
            )
        )
    ]
    for load in loads:
        load.start()

    def name(p, carry):
        slot = slot_ref[p]
        which = lax.rem(list_ref[slot // LISTED_COUNT, lax.rem(slot, LISTED_COUNT)], blocks)
        id_own[p // ZS, pl.ds(lax.rem(p, ZS), 1), :] = jnp.full((1, 128), which, jnp.int32)
        return carry

    lax.fori_loop(0, XS * CS * ZS, name, 0)
    counts = count_ref[...].astype(F32)
    capacity = there.out.shape[2]
    send_row = slot_rows(counts, me, capacity)
    recv_row = slot_rows(counts.T, me, capacity)
    kinds = upright(kind_ref[...])
    step = 256
    for load in loads[:2]:
        load.wait()
    for t in range(types):
        for k in range(units // step):
            cols = slice(t * units + k * step, t * units + (k + 1) * step)
            pre = dot_nn(x_ref[...], w1_ref[t, :, k * step : (k + 1) * step])
            keep = jnp.where(kinds == t, 1.0, 0.0)
            act, pull = jax.vjp(jax.nn.gelu, pre)
            hidden[:, cols] = (act * keep).astype(BF16)
            slope[:, cols] = pull(jnp.ones_like(pre))[0] * keep
    greeted()
    for load in loads[2:]:
        load.wait()
    for j in range(1, XS * CS):
        p, to = ret_v.peer(j)
        push(id_own.at[p], id_near.at[j - 1], id_send, id_recv, to)

    def prepare():
        pick_a[...] = pick_rows(upright(send_row), rows)
        pick_b[...] = pick_slots(recv_row, rows)

    def finish_there(total, h):
        own = x_ref[:, pl.ds(pl.multiple_of(y * share + h * half, half), half)]
        return (own.astype(F32) + total).astype(BF16)

    there.run(
        lambda g: dot_nn(hidden[...], w2_ref[:, span(g, share)]),
        finish_there, pick_a, pick_b, prepare,
    )
    for b in range(blocks):
        do_t[b] = head_rows(do_ref[b * BLOCK_ROWS : (b + 1) * BLOCK_ROWS, :].astype(F32)).astype(
            BF16
        )
    q, kv = 0.0, 0.0
    for h, g in there.parts():
        m = there.full[h, g]
        cols = pl.ds(pl.multiple_of(g * share + h * half, half), half)
        q = q + dot_nn(m, wq_ref[cols, :])
        kv = kv + dot_nt(wkv_ref[:, cols], m)
    kv = kv.astype(BF16)
    for b in range(blocks):
        cols = slice(b * BLOCK_ROWS, (b + 1) * BLOCK_ROWS)
        kvt[me * blocks + b] = kv[:, cols]
    for i in range(blocks_of.count()):
        blocks_of.event(i)
        if i == 0:
            q = q.astype(BF16).astype(F32) * SCALE
            for b in range(blocks):
                q_t[b] = head_rows(q[b * BLOCK_ROWS : (b + 1) * BLOCK_ROWS, :]).astype(BF16)
    blocks_of.finish()

    pieces = LISTED_COUNT // WIDE
    span_keys = WIDE * BLOCK_ROWS

    def listed(b, first, part):
        rows_of = slice(part * HEAD_SIZE, (part + 1) * HEAD_SIZE)
        return jnp.concatenate(
            [kvt[list_ref[b, first + k], rows_of, :] for k in range(WIDE)], axis=1
        )

    def soft(b, carry):
        base = b * LISTED_COUNT
        top = jnp.full((8, lanes), -jnp.inf, F32)
        for i in range(pieces):
            value = dot_tn(listed(b, i * WIDE, 0), q_t[b])
            score[i * span_keys : (i + 1) * span_keys, :] = value
            top = jnp.maximum(top, jnp.max(value.reshape(-1, 8, lanes), axis=0))
        top = jnp.max(top, axis=0, keepdims=True)
        total = jnp.zeros((8, lanes), F32)
        for i in range(pieces):
            value = jnp.exp(score[i * span_keys : (i + 1) * span_keys, :] - top)
            total = total + jnp.sum(value.reshape(-1, 8, lanes), axis=0)
            prob[b, i * span_keys : (i + 1) * span_keys, :] = value.astype(BF16)
        inverse = 1.0 / jnp.sum(total, axis=0, keepdims=True)
        stat[b] = jnp.broadcast_to(inverse, (8, lanes))
        scaled = (do_t[b].astype(F32) * inverse).astype(BF16)
        for i in range(pieces):
            grad = dot_nt(scaled, prob[b, i * span_keys : (i + 1) * span_keys, :]).astype(BF16)
            for k in range(WIDE):
                glist[base + i * WIDE + k] = grad[:, k * BLOCK_ROWS : (k + 1) * BLOCK_ROWS]
        return carry

    lax.fori_loop(0, blocks, soft, 0)

    def reorder(ref):
        def one(i, carry):
            ref[i] = glist[slot_ref[i]]
            return carry

        lax.fori_loop(0, ref.shape[0], one, 0, unroll=8)

    reorder(ret_v.g)
    ret_v.start()
    wait(id_near, id_recv)
    wait(id_own.at[pl.ds(0, XS * CS - 1)], id_send)

    def grads(b, carry):
        base = b * LISTED_COUNT
        acc = jnp.zeros((HEAD_SIZE, lanes), F32)
        for i in range(pieces):
            acc = acc + dot_nn(
                listed(b, i * WIDE, 1), prob[b, i * span_keys : (i + 1) * span_keys, :]
            )
        for k in range(1, blocks):
            pl.when(b == k)(functools.partial(ret_v.combine, k - 1))
        inverse = stat[b, 0:1, :]
        out_t = acc * inverse
        where = pl.ds(pl.multiple_of(b * BLOCK_ROWS, BLOCK_ROWS), BLOCK_ROWS)
        att_ref[where, :] = head_columns(out_t).astype(BF16)
        d = do_t[b]
        delta = jnp.sum(out_t * d.astype(F32), axis=0, keepdims=True)
        acc = jnp.zeros((HEAD_SIZE, lanes), F32)
        for i in range(pieces):
            p = prob[b, i * span_keys : (i + 1) * span_keys, :].astype(F32) * inverse
            dp = dot_tn(listed(b, i * WIDE, 1), d)
            ds = (p * (dp - delta)).astype(BF16)
            acc = acc + dot_nn(listed(b, i * WIDE, 0), ds)
            grad = dot_nt(q_t[b], ds).astype(BF16)
            for k in range(WIDE):
                glist[base + i * WIDE + k] = grad[:, k * BLOCK_ROWS : (k + 1) * BLOCK_ROWS]
        dq[where, :] = head_columns(acc * SCALE).astype(BF16)
        return carry

    lax.fori_loop(0, blocks, grads, 0)
    reorder(ret_k.g)
    ret_k.start()
    for i in range(blocks - 1, ZS - 1):
        ret_v.combine(i)
    total = ret_v.combine(ZS - 1)
    for i in range(4):
        ret_k.combine(i)
    total = ret_v.finish(total)
    kv_grad[:, HEAD_SIZE:] = total.T.astype(BF16)
    for i in range(4, ZS - 1):
        ret_k.combine(i)

    def kept_rows(g):
        return span(g, rows)

    for g in range(YS):
        cols = slice(g * share, (g + 1) * share)
        score[g * rows : (g + 1) * rows, :share] = dot_nt(dq[...], wq_ref[cols, :])
    pick_a[...] = pick_rows(upright(recv_row), rows)
    pick_b[...] = pick_slots(send_row, rows)
    total = ret_k.finish(ret_k.combine(ZS - 1))
    kv_grad[:, :HEAD_SIZE] = total.T.astype(BF16)

    def back_part(g):
        cols = span(g, share)
        return score[kept_rows(g), :share] + dot_nn(kv_grad[...], wkv_ref[:, cols])

    back.run(back_part, lambda total, h: total.astype(BF16), pick_a, pick_b)
    seen = 0
    for h, g in back.parts():
        seen += 1
        if seen < (h + 1) * YS:
            continue
        for k in range(types * units // step):
            cols = slice(k * step, (k + 1) * step)
            kept = (
                slice(k // 2 * rows, (k // 2 + 1) * rows), slice(k % 2 * step, (k % 2 + 1) * step)
            )
            grad = score[kept] if h else 0.0
            for group in range(YS):
                at = group * share + h * half
                grad = grad + dot_nt(back.full[h, group], w2_ref[cols, at : at + half])
            if h + 1 < HALVES:
                score[kept] = grad
            else:
                hidden[:, cols] = (grad * slope[:, cols]).astype(BF16)

    def inputs(g):
        part = 0.0
        for t in range(types):
            part = part + dot_nt(hidden[:, t * units : (t + 1) * units], w1_ref[t, span(g, share), :])
        return part

    last.start(inputs)
    for h in range(HALVES):
        last.relay(h)
    for h in range(HALVES):
        total = last.finish(h)
        value = back.full[h, y].astype(F32) + total
        out_ref[:, h * half : (h + 1) * half] = value.astype(BF16)
    last.drain()


VM = pl.BlockSpec(memory_space=pltpu.VMEM)
SM = pl.BlockSpec(memory_space=pltpu.SMEM)
HB = pl.BlockSpec(memory_space=pl.ANY)
DMA = pltpu.SemaphoreType.DMA


def run(lists, slots, x, kinds, do, w1, w2, wq, wkv, counts):
    rows, width = x.shape
    share = width // YS
    half = share // HALVES
    capacity = 2 * rows // PEERS
    blocks = rows // BLOCK_ROWS
    count = blocks * LISTED_COUNT
    lanes = GROUP_HEADS * BLOCK_ROWS
    tile = (HEAD_SIZE, BLOCK_ROWS)
    spread = [
        pltpu.VMEM((HALVES, YS - 1, rows, half), BF16),
        pltpu.VMEM((HALVES, YS - 1, rows, half), BF16),
    ]
    pairs = [DMA((HALVES, YS - 1)), DMA((HALVES, YS - 1))]
    handover = spread + [
        pltpu.VMEM((HALVES, PEERS, capacity, half), BF16),
        pltpu.VMEM((HALVES, PEERS, capacity, half), BF16),
        pltpu.VMEM((HALVES, YS, rows, half), BF16),
    ] + pairs + [DMA((HALVES,)), DMA((HALVES,))] + pairs
    back = [
        pltpu.VMEM((count,) + tile, BF16),
        pltpu.VMEM((ZS, XS * CS - 1) + tile, BF16),
        pltpu.VMEM((ZS - 1, blocks) + tile, BF16),
        pltpu.VMEM((ZS - 1, blocks) + tile, BF16),
        DMA,
        DMA((ZS,)),
        DMA,
        DMA((ZS - 1,)),
    ]
    return pl.pallas_call(
        kernel,
        out_shape=(
            jax.ShapeDtypeStruct((rows, share), BF16),
            jax.ShapeDtypeStruct((rows, share), BF16),
        ),
        in_specs=[SM, SM, HB, VM] + [HB] * 5 + [VM],
        out_specs=(VM, VM),
        scratch_shapes=[pltpu.VMEM(v.shape, BF16) for v in (x, do, w1, w2, wq, wkv)]
        + [
            DMA((6,)),
            pltpu.VMEM((rows, w2.shape[0]), BF16),
            pltpu.VMEM((rows, w2.shape[0]), F32),
            pltpu.VMEM((PEERS * capacity, rows), BF16),
            pltpu.VMEM((rows, PEERS * capacity), BF16),
            pltpu.VMEM((blocks, HEAD_SIZE, lanes), BF16),
            pltpu.VMEM((blocks, HEAD_SIZE, lanes), BF16),
            pltpu.VMEM((PEERS * blocks, 2 * HEAD_SIZE, BLOCK_ROWS), BF16),
            pltpu.VMEM((LISTED_COUNT * BLOCK_ROWS, lanes), F32),
            pltpu.VMEM((blocks, LISTED_COUNT * BLOCK_ROWS, lanes), BF16),
            pltpu.VMEM((count,) + tile, BF16),
            pltpu.VMEM((blocks, 8, lanes), F32),
            pltpu.VMEM((rows, share), BF16),
            pltpu.VMEM((rows, 2 * HEAD_SIZE), BF16),
            pltpu.VMEM((XS * CS, ZS, 128), jnp.int32),
            pltpu.VMEM((XS * CS - 1, ZS, 128), jnp.int32),
        ]
        + handover
        + handover
        + [DMA, DMA((PEERS,))]
        + [DMA, DMA]
        + back
        + back
        + [
            pltpu.VMEM((HALVES, rows, half), BF16),
            pltpu.VMEM((HALVES, rows, half), BF16),
            pltpu.VMEM((HALVES, 2, rows, half), BF16),
            pltpu.VMEM((HALVES, 2, rows, half), BF16),
            pltpu.VMEM((2, rows // 2, share), F32),
            DMA((HALVES, 2)),
            DMA((HALVES, 2)),
            DMA((HALVES, 2, 2)),
            DMA((HALVES, 2, 2)),
        ],
        compiler_params=pltpu.CompilerParams(
            collective_id=1, has_side_effects=True, vmem_limit_bytes=63 << 20
        ),
        name="step",
    )(
        lists, slots, x, kinds, do, w1, w2, wq, wkv, counts,
    )


def deliver_kernel(a_ref, b_ref, a_out, b_out):
    a_out[...] = a_ref[...]
    b_out[...] = b_ref[...]


def deliver(a, b):
    return pl.pallas_call(
        deliver_kernel,
        out_shape=tuple(jax.ShapeDtypeStruct(v.shape, v.dtype) for v in (a, b)),
        grid=(2,),
        in_specs=[pl.BlockSpec((a.shape[0] // 2, a.shape[1]), lambda i: (i, 0))] * 2,
        out_specs=(pl.BlockSpec((a.shape[0] // 2, a.shape[1]), lambda i: (i, 0)),) * 2,
        name="deliver",
    )(a, b)


def shards(
    elements,
    element_types,
    handover_counts,
    block_lists,
    w_first,
    w_second,
    w_query,
    key_value_weight,
    attention_cotangent,
):
    row_count, width = elements.shape
    types, units = w_second.shape[:2]
    blocks = row_count // BLOCK_ROWS
    slots = blocks * LISTED_COUNT
    spot = jnp.arange(slots, dtype=jnp.int32)[:, None, None]
    owner = (spot // ZS // CS * ZS + spot % ZS) * CS + spot // ZS % CS
    listed = block_lists[None]
    slot_of = jnp.sum(
        jnp.where(
            (listed >= owner * blocks) & (listed < (owner + 1) * blocks),
            jnp.arange(slots, dtype=jnp.int32).reshape(1, blocks, LISTED_COUNT),
            0,
        ),
        axis=(1, 2),
        dtype=jnp.int32,
    )
    w2 = w_second.reshape(types * units, width)
    kv_weight = key_value_weight.transpose(1, 2, 0).reshape(2 * HEAD_SIZE, width)
    attended, x_grad = run(
        block_lists, slot_of, elements, element_types[None, :], attention_cotangent, w_first, w2,
        w_query, kv_weight, handover_counts,
    )
    return deliver(attended, x_grad)


def solution(mesh):
    return jax.shard_map(
        shards,
        mesh=mesh,
        in_specs=(
            P("det", None),
            P("det"),
            P(),
            P("det", None),
            P(None, None, "head"),
            P(None, "head", None),
            P(None, "head"),
            P(None, None, "head"),
            P("det", "head"),
        ),
        out_specs=(P("det", "head"), P("det", "head")),
        check_vma=False,
    )
```
